32 devices in a mesh: wide: 8 (over z, y), narrow: 4 (over x, core).
Axes of the slice: x: 2, y: 2, z: 4, core: 2. Of those that a mesh axis runs over, the one named last changes fastest.
Arguments:
- left_edge: bfloat16 [448, 49, 448], P('wide', None, 'narrow'), may hold values from -40 to 40
- corner: bfloat16 [448, 448], P('narrow'), may hold values from -0.25 to 0.25
- right_edge: bfloat16 [448, 49, 448], P('wide', None, 'narrow'), may hold values from -0.25 to 0.25
- single_layer: bfloat16 [2, 2401], replicated, may hold values from -0.71875 to 0.71875
- warm_basis: bfloat16 [49, 448, 448], P(None, 'narrow', 'wide'), may hold values from -0.0390625 to 0.0390625
Outputs:
- new_basis: float32 [448, 49, 448], P('wide', None, 'narrow')
- r_factor: float32 [448, 448], replicated
The draws below stay inside these ranges and needn't reach their ends.
All inputs are finite; a program needn't handle non-finite values.
Results may differ from the reference program's by a relative error of at most 0.014.
Values may be sent and summed in bfloat16 or wider, within the bound.
No kernel may reach another device: no remote copies, remote signals or barrier semaphores. Data moves between devices by JAX's collectives and lax.ppermute only.
A program may use at most 192 MiB of HBM per device.

```python
import math
import jax
import jax.numpy as jnp
from jax import lax

BOND = 7
PHYS = 2
CHI = 448
DD = 49
N_WIDE = 8


def draw_left_edge(key, part):
    first, second = jax.random.split(key, 2)
    scales = jnp.exp(jax.random.uniform(first, (CHI, 1, 1), jnp.float32) * math.log(10.0))
    base = jnp.clip(jax.random.normal(second, (CHI, DD, CHI), jnp.float32), -4.0, 4.0)
    return (base * scales).astype(jnp.bfloat16)


def block_levels(own_key, dims, shards, least, top_value):
    loudness = 1.0
    for axis_at, parts in shards:
        heights = jax.random.uniform(jax.random.fold_in(jax.random.fold_in(own_key, 6), axis_at), (parts,), jnp.float32, least / len(shards), top_value / len(shards))
        loudness = loudness * jnp.repeat(jnp.exp(heights), dims[axis_at] // parts).reshape((-1,) + (1,) * (len(dims) - 1 - axis_at))
    return loudness


def centred(key, extent, deviation, most, cuts=(), kind=jnp.bfloat16):
    array = deviation * jax.random.normal(key, extent, jnp.float32)
    if cuts:
        array = array * block_levels(key, extent, cuts, -0.22, 0.18)
    return jnp.clip(array, -most, most).astype(kind)


def setup_inputs(seed: int = 0) -> dict:
    key_list = jax.random.split(jax.random.key(seed), 6)
    left_edge = draw_left_edge(jax.random.fold_in(key_list[5], 71), 0)
    corner = centred(key_list[1], (CHI, CHI), CHI ** -0.5, 0.25, ((0, 4),))
    right_edge = centred(key_list[2], (CHI, DD, CHI), CHI ** -0.5, 0.25, ((0, 8), (2, 4)))
    single_layer = centred(key_list[3], (PHYS, DD * DD), 0.12, 0.71875)
    warm_basis = centred(key_list[4], (DD, CHI, CHI), (DD * CHI) ** -0.5, 0.0390625, ((1, 4), (2, 8)))
    return dict(left_edge=left_edge, corner=corner, right_edge=right_edge, single_layer=single_layer, warm_basis=warm_basis)


def reference(left_edge, corner, right_edge, single_layer, warm_basis):
    layer = single_layer.astype(jnp.float32).reshape(PHYS, BOND, BOND, BOND, BOND)
    half_left = jnp.dot(left_edge.reshape(CHI * DD, CHI).astype(jnp.float32), corner.astype(jnp.float32), preferred_element_type=jnp.float32).astype(jnp.bfloat16)
    block = CHI // N_WIDE
    side_matrix = right_edge.reshape(CHI, DD * CHI)
    basis_matrix = warm_basis.reshape(DD * CHI, CHI)

    def one_block(rows_block):
        strip = jnp.dot(rows_block.reshape(block * DD, CHI).astype(jnp.float32), side_matrix.astype(jnp.float32), preferred_element_type=jnp.float32)
        strip = strip.astype(jnp.bfloat16).astype(jnp.float32).reshape(block, BOND, BOND, BOND, BOND, CHI)
        ket_layer = jnp.einsum('iuvlmj,suldr->ivmsdrj', strip, layer)
        enlarged = jnp.einsum('ivmsdrj,svmew->iderwj', ket_layer, layer)
        enlarged = enlarged.astype(jnp.bfloat16).reshape(block * DD, DD * CHI)
        return jnp.dot(enlarged.astype(jnp.float32), basis_matrix.astype(jnp.float32), preferred_element_type=jnp.float32)
    projected = lax.map(one_block, half_left.reshape(CHI // block, block, DD, CHI)).reshape(CHI * DD, CHI)
    gram = jnp.dot(projected.T.astype(jnp.float32), projected.astype(jnp.float32), precision=lax.Precision.HIGHEST, preferred_element_type=jnp.float32) / (CHI * DD)
    lower = jnp.linalg.cholesky(gram)
    solved = lax.linalg.triangular_solve(lower, projected.T, left_side=True, lower=True)
    return (solved.T.reshape(CHI, DD, CHI), lower.T)
```

```python
import functools
import jax
import jax.numpy as jnp
from jax import lax
from jax.experimental import pallas as pl
from jax.experimental.pallas import tpu as pltpu
from jax.sharding import PartitionSpec as P

BOND = 7
LANES = 128
BLOCK = 128
PANEL = 8
F32 = jnp.float32
BF16 = jnp.bfloat16
HIGHEST = lax.Precision.HIGHEST


def site_operands(single_layer):
    phys = single_layer.shape[0]
    layer = single_layer.reshape(phys, BOND, BOND, BOND, BOND)
    half = 4
    padded = jnp.pad(layer, ((0, 0), (0, 1), (0, 0), (0, 0), (0, 0)))
    eye = jnp.eye(half, dtype=layer.dtype)
    first = padded.transpose(3, 4, 0, 2, 1)[:, :, :, None, :, None, :] * eye[None, None, None, :, None, :, None]
    first = first.reshape(BOND * BOND * phys * half, BOND * half * 8)
    split = padded.reshape(phys, 2, half, BOND, BOND, BOND)
    second = jnp.pad(split.transpose(5, 4, 3, 1, 0, 2), ((0, 0), (0, 1), (0, 0), (0, 0), (0, 0), (0, 0)))
    return first, second.reshape(BOND * 8, BOND * 2 * phys * half)


def assemble(order_ref, pieces, stage, target, sems):
    count = len(pieces)
    copies = [pltpu.make_async_copy(piece, stage.at[s], sems.at[s]) for s, piece in enumerate(pieces)]
    for copy in copies:
        copy.start()
    target[...] = jnp.zeros_like(target)
    for copy in copies:
        copy.wait()
    _, square, depth, breadth = stage.shape

    def fill(q, carry):
        lane = pl.ds(pl.multiple_of(q * LANES, LANES), breadth)
        if count == 1:
            target[:, lane] = stage[0, q]
        for pair in range(count // 2):
            joined = jnp.concatenate(
                [stage[order_ref[2 * pair + k], q].astype(F32) for k in range(2)], axis=0)
            target[pl.ds(pair * 2 * depth, 2 * depth), lane] = joined.astype(BF16)
        return carry
    lax.fori_loop(0, square, fill, 0)


def enlarge_kernel(parts_of, count, order_ref, *refs):
    left_refs, corner_refs = refs[:parts_of], refs[parts_of:2 * parts_of]
    first_ref, second_ref = refs[2 * parts_of:2 * parts_of + 2]
    rest = refs[2 * parts_of + 2:]
    if count:
        pieces, (out_ref, right_all, stage, strip, ket, sems) = rest[:count], rest[count:]

        @pl.when(pl.program_id(0) == 0)
        def _():
            assemble(order_ref, pieces, stage, right_all, sems)
    else:
        right_all, out_ref, strip, ket = rest
    rows = left_refs[0].shape[0]
    square = BOND * BOND
    span = BOND * LANES

    half_left = jnp.dot(left_refs[0][...], corner_refs[0][...], preferred_element_type=F32)
    for n in range(1, parts_of):
        half_left += jnp.dot(left_refs[n][...], corner_refs[n][...], preferred_element_type=F32)
    half_left = half_left.astype(BF16)
    for l in range(BOND):
        strip[l] = jnp.dot(half_left, right_all[:, l * span:(l + 1) * span], preferred_element_type=F32).astype(BF16)

    def one_pair(pair, carry):
        for i in range(2):
            parts = []
            for g in range(2):
                at = pl.ds(pl.multiple_of((pair * 2 + i) * 64 + g * 32, 32), 32)
                data = strip[:, at, :].reshape(BOND * 32, span)
                part = jnp.dot(first_ref[...], data, preferred_element_type=F32)
                parts.append(part.reshape(square, 8, span))
            ket[i] = jnp.concatenate(parts, axis=1).astype(BF16)
        for d in range(BOND):
            rows_of = []
            for lp in range(BOND):
                rows_of.append(jnp.concatenate(
                    [ket[i, d * BOND + r, :, lp * LANES:(lp + 1) * LANES] for r in range(BOND) for i in range(2)],
                    axis=1))
            data = jnp.concatenate(rows_of, axis=0)
            value = jnp.dot(second_ref[...], data, preferred_element_type=F32)
            at = pl.ds(pl.multiple_of((pair * BOND + d) * 16, 16), 16)
            for r in range(BOND):
                two = [value[:, (r * 2 + i) * LANES:(r * 2 + i + 1) * LANES].reshape(BOND, 8, LANES)
                       for i in range(2)]
                both = jnp.concatenate(two, axis=1).astype(BF16)
                for rp in range(BOND):
                    out_ref[at, (r * BOND + rp) * LANES:(r * BOND + rp + 1) * LANES] = both[rp]
        return carry
    lax.fori_loop(0, rows // 128, one_pair, 0)


def whole_block(a):
    return pl.BlockSpec(a.shape, lambda s: (0,) * a.ndim, pipeline_mode=pl.Buffered(1))


ROWS = 512


def enlarge(lefts, corners, right, order, first, second, begin, steps):
    depth = lefts[0].shape[1]
    pieces = right if isinstance(right, list) else None
    square = BOND * BOND
    lanes = square * LANES
    out_rows = ROWS // 128 * BOND * 16
    in_specs = [pl.BlockSpec(memory_space=pltpu.SMEM)]
    in_specs += [pl.BlockSpec((ROWS, depth), lambda s: (s + begin, 0))] * len(lefts)
    in_specs += [whole_block(c) for c in corners] + [whole_block(first), whole_block(second)]
    out_specs = [pl.BlockSpec((out_rows, lanes), lambda s: (s, 0))]
    out_shape = [jax.ShapeDtypeStruct((steps * out_rows, lanes), BF16)]
    scratch = [pltpu.VMEM((BOND, ROWS, BOND * LANES), BF16), pltpu.VMEM((2, square, 16, BOND * LANES), BF16)]
    if pieces:
        width = len(pieces) * pieces[0].shape[1]
        in_specs += [pl.BlockSpec(memory_space=pl.ANY)] * len(pieces)
        out_specs.append(pl.BlockSpec((width, lanes), lambda s: (0, 0), pipeline_mode=pl.Buffered(1)))
        out_shape.append(jax.ShapeDtypeStruct((width, lanes), BF16))
        scratch = [pltpu.VMEM((len(pieces),) + pieces[0].shape, BF16)] + scratch
        scratch.append(pltpu.SemaphoreType.DMA((len(pieces),)))
    else:
        in_specs.append(whole_block(right))
    flops = 2 * steps * ROWS * lanes * 1024
    return pl.pallas_call(
        functools.partial(enlarge_kernel, len(lefts), len(pieces) if pieces else 0),
        grid=(steps,),
        in_specs=in_specs,
        out_specs=out_specs,
        out_shape=out_shape,
        scratch_shapes=scratch,
        compiler_params=pltpu.CompilerParams(dimension_semantics=("arbitrary",), vmem_limit_bytes=60 << 20),
        cost_estimate=pl.CostEstimate(flops=flops, transcendentals=0, bytes_accessed=steps * out_rows * lanes * 2),
        name="enlarge",
    )(order, *lefts, *corners, first, second, *(pieces if pieces else [right]))


def project_kernel(count, order_ref, *refs):
    begins, parts = count
    rows_refs, pieces = refs[:len(begins)], refs[len(begins):len(begins) + parts]
    out_ref, stage, basis_all, sems = refs[len(begins) + parts:]
    step = pl.program_id(0)

    @pl.when(step == 0)
    def _():
        assemble(order_ref, pieces, stage, basis_all, sems)

    for which, (begin, steps) in enumerate(begins):
        @pl.when((step >= begin) & (step < begin + steps))
        def _():
            out_ref[...] = lax.dot_general(rows_refs[which][...], basis_all[...], (((1,), (1,)), ((), ())),
                                           preferred_element_type=F32).astype(out_ref.dtype)


def project(enlarged, pieces, order):
    lanes = enlarged[0].shape[1]
    rows = ROWS // 128 * BOND * 16
    steps = [e.shape[0] // rows for e in enlarged]
    begins = [(sum(steps[:n]), steps[n]) for n in range(len(steps))]
    width = len(pieces) * pieces[0].shape[1]
    part = lambda begin, count: pl.BlockSpec((rows, lanes), lambda s: (jnp.clip(s - begin, 0, count - 1), 0))
    return pl.pallas_call(
        functools.partial(project_kernel, (begins, len(pieces))),
        grid=(sum(steps),),
        in_specs=[pl.BlockSpec(memory_space=pltpu.SMEM)] + [part(*b) for b in begins]
        + [pl.BlockSpec(memory_space=pl.ANY)] * len(pieces),
        out_specs=pl.BlockSpec((rows, width), lambda s: (s, 0)),
        out_shape=jax.ShapeDtypeStruct((sum(steps) * rows, width), BF16),
        scratch_shapes=[pltpu.VMEM((len(pieces),) + pieces[0].shape, BF16), pltpu.VMEM((width, lanes), BF16),
                        pltpu.SemaphoreType.DMA((len(pieces),))],
        compiler_params=pltpu.CompilerParams(dimension_semantics=("arbitrary",), vmem_limit_bytes=61 << 20),
        name="project",
    )(order, *enlarged, *pieces)


def factor_kernel(real, gram_ref, upper_ref, inverse_ref, work, cell):
    size = gram_ref.shape[0]
    blocks = size // BLOCK
    lane = lax.broadcasted_iota(jnp.int32, (BLOCK, size), 1)
    row = lax.broadcasted_iota(jnp.int32, (BLOCK, size), 0)
    for k in range(blocks):
        unit = (lane == row + k * BLOCK).astype(F32)
        work[k, :, :size] = gram_ref[k * BLOCK:(k + 1) * BLOCK, :] + jnp.where(lane >= real, unit, 0.0)
        work[k, :, size:] = unit
    sub = lax.broadcasted_iota(jnp.int32, (PANEL, BLOCK), 0)
    lane8 = lax.broadcasted_iota(jnp.int32, (PANEL, BLOCK), 1)
    panels = BLOCK // PANEL

    def block_step(k, carry):
        here = pl.ds(pl.multiple_of(k * BLOCK, BLOCK), BLOCK)
        cell[:, :BLOCK] = work[k, :, here]
        row_b = lax.broadcasted_iota(jnp.int32, (BLOCK, BLOCK), 0)
        lane_b = lax.broadcasted_iota(jnp.int32, (BLOCK, BLOCK), 1)
        cell[:, BLOCK:] = (row_b == lane_b).astype(F32)
        for p in range(panels):
            base = p * PANEL
            left = cell[base:base + PANEL, :BLOCK]
            right = cell[base:base + PANEL, BLOCK:]
            spread = [jnp.broadcast_to(left[:, base + t:base + t + 1], (PANEL, BLOCK)) for t in range(PANEL)]
            scale = jnp.zeros((PANEL, BLOCK), F32)
            for t in range(PANEL):
                inv = 1.0 / jnp.broadcast_to(spread[t][t:t + 1, :], (PANEL, BLOCK))
                factor = jnp.where(sub > t, spread[t] * inv, 0.0)
                scale = jnp.where(sub == t, inv, scale)
                for later in range(t + 1, PANEL):
                    spread[later] = spread[later] - factor * jnp.broadcast_to(
                        spread[later][t:t + 1, :], (PANEL, BLOCK))
                left = left - factor * jnp.broadcast_to(left[t:t + 1, :], (PANEL, BLOCK))
                right = right - factor * jnp.broadcast_to(right[t:t + 1, :], (PANEL, BLOCK))
            weights = jnp.transpose(left * scale)
            for g in range(p + 1, panels):
                at = slice(g * PANEL, (g + 1) * PANEL)
                a, b = cell[at, :BLOCK], cell[at, BLOCK:]
                for t in range(PANEL):
                    w = jnp.broadcast_to(weights[at, t:t + 1], (PANEL, BLOCK))
                    a = a - w * jnp.broadcast_to(left[t:t + 1, :], (PANEL, BLOCK))
                    b = b - w * jnp.broadcast_to(right[t:t + 1, :], (PANEL, BLOCK))
                cell[at, :BLOCK] = a
                cell[at, BLOCK:] = b
            root = jnp.sqrt(scale)
            cell[base:base + PANEL, BLOCK:] = right * root
        low = cell[:, BLOCK:]
        mine = jnp.dot(low, work[k], precision=HIGHEST, preferred_element_type=F32)
        work[k] = mine

        def update(i, c):
            there = pl.ds(pl.multiple_of(i * BLOCK, BLOCK), BLOCK)
            work[i] = work[i] - lax.dot_general(work[k, :, there], mine, (((0,), (0,)), ((), ())),
                                                precision=HIGHEST, preferred_element_type=F32)
            return c
        lax.fori_loop(k + 1, blocks, update, 0)
        return carry
    lax.fori_loop(0, blocks, block_step, 0)
    for k in range(blocks):
        at = slice(k * BLOCK, (k + 1) * BLOCK)
        upper_ref[at, :] = jnp.where(lane >= row + k * BLOCK, work[k, :, :size], 0.0)
        inverse_ref[at, :] = work[k, :, size:]


def factorize(gram, real):
    size = gram.shape[0]
    return pl.pallas_call(
        functools.partial(factor_kernel, real),
        out_shape=(jax.ShapeDtypeStruct((size, size), F32),) * 2,
        scratch_shapes=[pltpu.VMEM((size // BLOCK, BLOCK, 2 * size), F32), pltpu.VMEM((BLOCK, 2 * BLOCK), F32)],
        compiler_params=pltpu.CompilerParams(vmem_limit_bytes=60 << 20),
        name="factor",
    )(gram)


def solve_kernel(count, order_ref, low_ref, *refs):
    pieces, out_ref = refs[:count], refs[count]
    low = low_ref[...]
    terms = []
    for _ in range(3):
        term = low.astype(BF16)
        low = low - term.astype(F32)
        terms.append(term)
    for which in range(count):
        @pl.when(pl.program_id(0) == which)
        def _():
            data = pieces[which][...]
            value = sum(lax.dot_general(data, term, (((1,), (1,)), ((), ())), preferred_element_type=F32)
                        for term in terms)
            pairs = data.shape[0] // (BOND * 16)
            value = value.reshape(pairs, BOND, 2, 8, value.shape[1])
            for pair in range(pairs):
                for d in range(BOND):
                    for i in range(2):
                        out_ref[pair * 2 + i, d * BOND:(d + 1) * BOND, :] = value[pair, d, i, :BOND, :]


def solve(pieces, low, order):
    rows, width = pieces[0].shape
    outer = rows // (BOND * 8)
    cols = low.shape[0]
    full = lambda shape: pl.BlockSpec(shape, lambda s, order: (0,) * len(shape))
    return pl.pallas_call(
        functools.partial(solve_kernel, len(pieces)),
        grid_spec=pltpu.PrefetchScalarGridSpec(
            num_scalar_prefetch=1, grid=(len(pieces),),
            in_specs=[full(low.shape)] + [full((rows, width))] * len(pieces),
            out_specs=pl.BlockSpec((outer, BOND * BOND, cols), lambda s, order: (order[s], 0, 0))),
        out_shape=jax.ShapeDtypeStruct((outer * len(pieces), BOND * BOND, cols), F32),
        compiler_params=pltpu.CompilerParams(dimension_semantics=("arbitrary",), vmem_limit_bytes=60 << 20),
        name="solve",
    )(order, low, *pieces)


def swap(x, axis, mask):
    count = lax.axis_size(axis)
    return lax.ppermute(x, axis, [(i, i ^ mask) for i in range(count)])


def gather_blocks(x, axis):
    count = lax.axis_size(axis)
    if count != 8:
        whole = lax.all_gather(x, axis, axis=1, tiled=True)
        return [whole]
    blocks = {0: x, 1: swap(x, axis, 1), 2: swap(x, axis, 2), 6: swap(x, axis, 6)}
    blocks[3] = swap(blocks[2], axis, 1)
    blocks[4] = swap(blocks[6], axis, 2)
    blocks[7] = swap(blocks[1], axis, 6)
    blocks[5] = swap(blocks[4], axis, 1)
    return [blocks[m] for m in range(count)]


def gather_few(x, axis):
    blocks = [x]
    for bit in reversed(range(lax.axis_size(axis).bit_length() - 1)):
        blocks = blocks + [swap(b, axis, 1 << bit) for b in blocks]
    return blocks


def reversed_masks(count):
    masks = [0]
    for bit in reversed(range(count.bit_length() - 1)):
        masks = masks + [m | (1 << bit) for m in masks]
    return masks


def split_sum(x, axis, mask):
    upper = (lax.axis_index(axis) & mask) > 0
    half = x.shape[0] // 2
    keep = jnp.where(upper, x[half:], x[:half])
    send = jnp.where(upper, x[:half], x[half:])
    return (keep.astype(F32) + swap(send, axis, mask).astype(F32)).astype(x.dtype)


def join(x, axis, mask):
    upper = (lax.axis_index(axis) & mask) > 0
    other = swap(x, axis, mask)
    return jnp.concatenate([jnp.where(upper, other, x), jnp.where(upper, x, other)])


def on_device(left_edge, corner, right_edge, single_layer, warm_basis):
    local_rows, square, depth = left_edge.shape
    breadth = corner.shape[1]
    local_cols = right_edge.shape[2]
    narrow = lax.axis_size("narrow")
    wide = lax.axis_size("wide")
    own = lax.axis_index("narrow")
    masks = reversed_masks(narrow)

    right = gather_blocks(right_edge.transpose(1, 0, 2), "wide")
    extra = -local_rows % 8
    left = left_edge.reshape(local_rows, BOND, BOND, depth).transpose(0, 2, 1, 3)
    left = jnp.pad(left, ((0, extra), (0, 1), (0, 1), (0, 0))).reshape((local_rows + extra) * 64, depth)
    lefts = gather_few(left, "narrow")
    corners = gather_few(corner, "narrow")
    order = jnp.arange(len(right), dtype=jnp.int32)
    if len(right) > 1:
        order = order ^ lax.axis_index("wide").astype(jnp.int32)
    first, second = site_operands(single_layer)

    basis_local, _ = lax.optimization_barrier((warm_basis.transpose(0, 2, 1), right[5] if len(right) > 1 else right[0]))
    basis = gather_blocks(basis_local, "wide")

    steps = lefts[0].shape[0] // ROWS
    cuts = [0, 3, 5, steps] if steps > 5 else [0, steps]
    enlarged = []
    for n in range(len(cuts) - 1):
        made = enlarge(lefts, corners, right, order, first, second, cuts[n], cuts[n + 1] - cuts[n])
        enlarged.append(made[0])
        if n == 0:
            right = made[1]
    rows = project(enlarged, basis, order)

    for bit in range(narrow.bit_length() - 1):
        rows = split_sum(rows, "narrow", 1 << bit)
    gram = lax.dot_general(rows, rows, (((0,), (0,)), ((), ())), preferred_element_type=F32) / (breadth * square)
    spare = -breadth % BLOCK
    gram = jnp.pad(gram, ((0, spare), (0, spare)))
    route = [("narrow", 1 << b) for b in range(narrow.bit_length() - 1)]
    route += [("wide", 1 << b) for b in range(wide.bit_length() - 1)]
    for axis, mask in route:
        gram = split_sum(gram, axis, mask)
    for axis, mask in reversed(route):
        gram = join(gram, axis, mask)
    upper, inverse = factorize(gram, breadth)

    pieces = gather_few(rows, "narrow")
    at = []
    for mask in masks:
        block = own ^ mask
        spot = 0
        for bit in range(narrow.bit_length() - 1):
            spot = spot * 2 + ((block >> bit) & 1)
        at.append(spot)
    low = lax.dynamic_slice(inverse, (own * local_cols, 0), (local_cols, breadth))
    new_basis = solve(pieces, low, jnp.stack(at).astype(jnp.int32))
    return new_basis[:local_rows], upper[:breadth, :breadth]


def solution(mesh):
    placed = (
        P("wide", None, "narrow"),
        P("narrow", None),
        P("wide", None, "narrow"),
        P(),
        P(None, "narrow", "wide"),
    )
    return jax.shard_map(
        on_device,
        mesh=mesh,
        in_specs=placed,
        out_specs=(P("wide", None, "narrow"), P()),
        check_vma=False,
    )
```

```python
import functools
import jax
import jax.numpy as jnp
from jax import lax
from jax.experimental import pallas as pl
from jax.experimental.pallas import tpu as pltpu
from jax.sharding import PartitionSpec as P


BOND = 7
LANES = 128
BLOCK = 128
PANEL = 8
ROWS = 512
OUTER = ROWS // 64
SPLIT = 7
F32 = jnp.float32
BF16 = jnp.bfloat16
HIGHEST = lax.Precision.HIGHEST


def site_operands(single_layer):
    phys = single_layer.shape[0]
    layer = single_layer.reshape(phys, BOND, BOND, BOND, BOND)
    half = 4
    padded = jnp.pad(layer, ((0, 0), (0, 1), (0, 0), (0, 0), (0, 0)))
    eye = jnp.eye(half, dtype=layer.dtype)
    first = padded.transpose(3, 4, 0, 2, 1)[:, :, :, None, :, None, :] * eye[None, None, None, :, None, :, None]
    first = first.reshape(BOND * BOND * phys * half, BOND * half * 8)
    split = padded.reshape(phys, 2, half, BOND, BOND, BOND)
    second = jnp.pad(split.transpose(5, 4, 3, 1, 0, 2), ((0, 0), (0, 1), (0, 0), (0, 0), (0, 0), (0, 0)))
    return first, second.reshape(BOND * 8, BOND * 2 * phys * half)


def assemble(layout, order_ref, pieces, stage, target, sems):
    copies = [pltpu.make_async_copy(piece, stage.at[block, pl.ds(begin, size)], sems.at[s])
              for s, ((block, begin, size), piece) in enumerate(zip(layout, pieces))]
    for copy in copies:
        copy.start()
    target[...] = jnp.zeros_like(target)
    for copy in copies:
        copy.wait()
    count, square, depth, breadth = stage.shape

    def fill(q, carry):
        lane = pl.ds(pl.multiple_of(q * LANES, LANES), breadth)
        if count == 1:
            target[:, lane] = stage[0, q]
        for pair in range(count // 2):
            joined = jnp.concatenate(
                [stage[order_ref[2 * pair + k], q].astype(F32) for k in range(2)], axis=0)
            target[pl.ds(pair * 2 * depth, 2 * depth), lane] = joined.astype(BF16)
        return carry

    lax.fori_loop(0, square, fill, 0)


def half_left_kernel(parts_of, *refs):
    left_refs, corner_refs = refs[:parts_of], refs[parts_of:2 * parts_of]
    out_ref, total, spread = refs[2 * parts_of:]
    value = jnp.dot(left_refs[0][...], corner_refs[0][...], preferred_element_type=F32)
    for n in range(1, parts_of):
        value += jnp.dot(left_refs[n][...], corner_refs[n][...], preferred_element_type=F32)
    outer = total.shape[0] // (BOND * BOND)
    spread[...] = jnp.zeros_like(spread)
    width = value.shape[1]
    total[:, :width] = value

    def place(u, v):
        begin = (u * BOND + v) * outer
        if outer % 8 == 0:
            begin = pl.multiple_of(begin, 8)
        for c in range(spread.shape[0]):
            data = total[pl.ds(begin, outer), c * LANES:(c + 1) * LANES]
            spread[c, pl.ds(v * 8 + u, outer, stride=64), :] = data

    if outer % 8 == 0:
        lax.fori_loop(0, BOND * BOND, lambda p, carry: (place(p // BOND, p % BOND), carry)[1], 0)
    else:
        for p in range(BOND * BOND):
            place(p // BOND, p % BOND)
    for c in range(spread.shape[0]):
        count = min(LANES, width - c * LANES)
        out_ref[:, c * LANES:c * LANES + count] = spread[c, :, :count].astype(BF16)


def half_left_of(lefts, corners, outer):
    width = corners[0].shape[1]
    return pl.pallas_call(
        functools.partial(half_left_kernel, len(lefts)),
        out_shape=jax.ShapeDtypeStruct((outer * 64, width), BF16),
        scratch_shapes=[pltpu.VMEM((lefts[0].shape[0], -(-width // LANES) * LANES), F32),
                        pltpu.VMEM((-(-width // LANES), outer * 64, LANES), F32)],
        compiler_params=pltpu.CompilerParams(vmem_limit_bytes=60 << 20),
        name="half_left",
    )(*lefts, *corners)


def enlarge_kernel(layout, order_ref, half_ref, first_ref, second_ref, *rest):
    count = len(layout)
    if count:
        pieces, (out_ref, right_all, stage, strip, ket, sems) = rest[:count], rest[count:]

        @pl.when(pl.program_id(0) == 0)
        def _():
            assemble(layout, order_ref, pieces, stage, right_all, sems)
    else:
        right_all, _, out_ref, strip, ket = rest
    rows = half_ref.shape[0]
    square = BOND * BOND
    span = BOND * LANES
    half_left = half_ref[...]
    for l in range(BOND):
        strip[l] = jnp.dot(half_left, right_all[:, l * span:(l + 1) * span], preferred_element_type=F32).astype(BF16)

    def one_pair(pair, carry):
        for i in range(2):
            parts = []
            for g in range(2):
                at = pl.ds(pl.multiple_of((pair * 2 + i) * 64 + g * 32, 32), 32)
                data = strip[:, at, :].reshape(BOND * 32, span)
                part = jnp.dot(first_ref[...], data, preferred_element_type=F32)
                parts.append(part.reshape(square, 8, span))
            ket[i] = jnp.concatenate(parts, axis=1).astype(BF16)
        for d in range(BOND):
            rows_of = []
            for lp in range(BOND):
                rows_of.append(jnp.concatenate(
                    [ket[i, d * BOND + r, :, lp * LANES:(lp + 1) * LANES] for r in range(BOND) for i in range(2)],
                    axis=1))
            data = jnp.concatenate(rows_of, axis=0)
            value = jnp.dot(second_ref[...], data, preferred_element_type=F32)
            at = pl.ds(pl.multiple_of((pair * BOND + d) * 16, 16), 16)
            for r in range(BOND):
                two = [value[:, (r * 2 + i) * LANES:(r * 2 + i + 1) * LANES].reshape(BOND, 8, LANES)
                       for i in range(2)]
                both = jnp.concatenate(two, axis=1).astype(BF16)
                for rp in range(BOND):
                    out_ref[at, (r * BOND + rp) * LANES:(r * BOND + rp + 1) * LANES] = both[rp]
        return carry

    lax.fori_loop(0, rows // 128, one_pair, 0)


def whole_block(a):
    return pl.BlockSpec(a.shape, lambda s: (0,) * a.ndim, pipeline_mode=pl.Buffered(1))


def shape_of(pieces):
    blocks = 1 + max(block for block, _, _ in pieces)
    square = sum(piece.shape[0] for block, _, piece in pieces if block == 0)
    return (blocks, square) + pieces[0][2].shape[1:]


def layout_of(pieces):
    return tuple((block, begin, piece.shape[0]) for block, begin, piece in pieces)


def enlarge(half_left, right, order, first, second, begin, steps, before=None):
    total, depth = half_left.shape
    pieces = right if isinstance(right, list) else None
    square = BOND * BOND
    lanes = square * LANES
    out_rows = ROWS // 128 * BOND * 16
    in_specs = [pl.BlockSpec(memory_space=pltpu.SMEM), pl.BlockSpec((ROWS, depth), lambda s: (s + begin, 0)),
                whole_block(first), whole_block(second)]
    out_specs = [pl.BlockSpec((out_rows, lanes), lambda s: (s + begin, 0))]
    out_shape = [jax.ShapeDtypeStruct((total // ROWS * out_rows, lanes), BF16)]
    scratch = [pltpu.VMEM((BOND, ROWS, BOND * LANES), BF16), pltpu.VMEM((2, square, 16, BOND * LANES), BF16)]
    if pieces:
        shape = shape_of(pieces)
        width = shape[0] * shape[2]
        in_specs += [pl.BlockSpec(memory_space=pl.ANY)] * len(pieces)
        out_specs.append(pl.BlockSpec((width, lanes), lambda s: (0, 0), pipeline_mode=pl.Buffered(1)))
        out_shape.append(jax.ShapeDtypeStruct((width, lanes), BF16))
        scratch = [pltpu.VMEM(shape, BF16)] + scratch
        scratch.append(pltpu.SemaphoreType.DMA((len(pieces),)))
    else:
        in_specs += [whole_block(right), pl.BlockSpec(memory_space=pl.ANY)]
    flops = 2 * steps * ROWS * lanes * 1024
    return pl.pallas_call(
        functools.partial(enlarge_kernel, layout_of(pieces) if pieces else ()),
        grid=(steps,),
        in_specs=in_specs,
        out_specs=out_specs,
        out_shape=out_shape,
        scratch_shapes=scratch,
        compiler_params=pltpu.CompilerParams(dimension_semantics=("arbitrary",), vmem_limit_bytes=60 << 20),
        cost_estimate=pl.CostEstimate(flops=flops, transcendentals=0, bytes_accessed=steps * out_rows * lanes * 2),
        input_output_aliases={} if pieces else {len(in_specs) - 1: 0},
        name="enlarge",
    )(order, half_left, first, second, *([p for _, _, p in pieces] if pieces else [right, before]))


def project_kernel(layout, order_ref, spot_ref, rows_ref, *refs):
    count = len(layout)
    if count:
        pieces, (out_ref, basis_all, stage, sems) = refs[:count], refs[count:]

        @pl.when(pl.program_id(0) == 0)
        def _():
            assemble(layout, order_ref, pieces, stage, basis_all, sems)
    else:
        basis_all, out_ref = refs
    out_ref[...] = lax.dot_general(rows_ref[...], basis_all[...], (((1,), (1,)), ((), ())),
                                   preferred_element_type=F32).astype(out_ref.dtype)


def project(enlarged, basis, order, spot, rows, width):
    lanes = enlarged.shape[1]
    pieces = basis if isinstance(basis, list) else None
    once = rows // SPLIT
    full = lambda shape: pl.BlockSpec(shape, lambda s, order, spot: (0,) * len(shape), pipeline_mode=pl.Buffered(1))
    in_specs = [pl.BlockSpec((once, lanes), lambda s, order, spot: (spot[0] * SPLIT + s, 0))]
    out_specs = [pl.BlockSpec((once, width), lambda s, order, spot: (s, 0))]
    out_shape = [jax.ShapeDtypeStruct((rows, width), BF16)]
    scratch = []
    if pieces:
        in_specs += [pl.BlockSpec(memory_space=pl.ANY)] * len(pieces)
        out_specs.append(full((width, lanes)))
        out_shape.append(jax.ShapeDtypeStruct((width, lanes), BF16))
        scratch += [pltpu.VMEM(shape_of(pieces), BF16), pltpu.SemaphoreType.DMA((len(pieces),))]
    else:
        in_specs.append(full(basis.shape))
    return pl.pallas_call(
        functools.partial(project_kernel, layout_of(pieces) if pieces else ()),
        grid_spec=pltpu.PrefetchScalarGridSpec(
            num_scalar_prefetch=2, grid=(SPLIT,), in_specs=in_specs, out_specs=out_specs, scratch_shapes=scratch),
        out_shape=out_shape,
        compiler_params=pltpu.CompilerParams(dimension_semantics=("arbitrary",), vmem_limit_bytes=60 << 20),
        cost_estimate=pl.CostEstimate(flops=2 * rows * width * lanes, transcendentals=0,
                                      bytes_accessed=2 * rows * lanes),
        name="project",
    )(order, spot, enlarged, *([p for _, _, p in pieces] if pieces else [basis]))


def factor_kernel(real, gram_ref, upper_ref, inverse_ref, work, cell):
    blocks = work.shape[0]
    size = blocks * BLOCK
    lane = lax.broadcasted_iota(jnp.int32, (BLOCK, size), 1)
    row = lax.broadcasted_iota(jnp.int32, (BLOCK, size), 0)
    place = 0
    for k in range(blocks):
        unit = (lane == row + k * BLOCK).astype(F32)
        work[k, :, :size] = jnp.where(lane >= real, unit, 0.0)
        work[k, :, size:] = unit
        for j in range(k, blocks):
            at = slice(j * BLOCK, (j + 1) * BLOCK)
            work[k, :, at] = work[k, :, at] + gram_ref[place * BLOCK:(place + 1) * BLOCK, :]
            place += 1
    sub = lax.broadcasted_iota(jnp.int32, (PANEL, BLOCK), 0)
    lane8 = lax.broadcasted_iota(jnp.int32, (PANEL, BLOCK), 1)
    panels = BLOCK // PANEL

    def block_step(k, carry):
        here = pl.ds(pl.multiple_of(k * BLOCK, BLOCK), BLOCK)
        cell[:, :BLOCK] = work[k, :, here]
        row_b = lax.broadcasted_iota(jnp.int32, (BLOCK, BLOCK), 0)
        lane_b = lax.broadcasted_iota(jnp.int32, (BLOCK, BLOCK), 1)
        cell[:, BLOCK:] = (row_b == lane_b).astype(F32)
        for p in range(panels):
            base = p * PANEL
            left = cell[base:base + PANEL, :BLOCK]
            right = cell[base:base + PANEL, BLOCK:]
            spread = [jnp.broadcast_to(left[:, base + t:base + t + 1], (PANEL, BLOCK)) for t in range(PANEL)]
            scale = jnp.zeros((PANEL, BLOCK), F32)
            for t in range(PANEL):
                inv = 1.0 / jnp.broadcast_to(spread[t][t:t + 1, :], (PANEL, BLOCK))
                factor = jnp.where(sub > t, spread[t] * inv, 0.0)
                scale = jnp.where(sub == t, inv, scale)
                for later in range(t + 1, PANEL):
                    spread[later] = spread[later] - factor * jnp.broadcast_to(
                        spread[later][t:t + 1, :], (PANEL, BLOCK))
                left = left - factor * jnp.broadcast_to(left[t:t + 1, :], (PANEL, BLOCK))
                right = right - factor * jnp.broadcast_to(right[t:t + 1, :], (PANEL, BLOCK))
            weights = jnp.transpose(left * scale)
            for g in range(p + 1, panels):
                at = slice(g * PANEL, (g + 1) * PANEL)
                a, b = cell[at, :BLOCK], cell[at, BLOCK:]
                for t in range(PANEL):
                    w = jnp.broadcast_to(weights[at, t:t + 1], (PANEL, BLOCK))
                    a = a - w * jnp.broadcast_to(left[t:t + 1, :], (PANEL, BLOCK))
                    b = b - w * jnp.broadcast_to(right[t:t + 1, :], (PANEL, BLOCK))
                cell[at, :BLOCK] = a
                cell[at, BLOCK:] = b
            root = jnp.sqrt(scale)
            cell[base:base + PANEL, BLOCK:] = right * root
        low = cell[:, BLOCK:]
        mine = jnp.dot(low, work[k], precision=HIGHEST, preferred_element_type=F32)
        work[k] = mine

        def update(i, c):
            there = pl.ds(pl.multiple_of(i * BLOCK, BLOCK), BLOCK)
            work[i] = work[i] - lax.dot_general(work[k, :, there], mine, (((0,), (0,)), ((), ())),
                                                precision=HIGHEST, preferred_element_type=F32)
            return c

        lax.fori_loop(k + 1, blocks, update, 0)
        return carry

    lax.fori_loop(0, blocks, block_step, 0)
    for k in range(blocks):
        count = min(BLOCK, real - k * BLOCK)
        at = slice(k * BLOCK, k * BLOCK + count)
        upper = jnp.where(lane >= row + k * BLOCK, work[k, :, :size], 0.0)
        upper_ref[at, :] = upper[:count, :real]
        inverse_ref[at, :] = work[k, :count, size:size + real]


def packed_blocks(gram):
    real = gram.shape[0]
    spare = -real % BLOCK
    gram = jnp.pad(gram, ((0, spare), (0, spare)))
    blocks = gram.shape[0] // BLOCK
    return jnp.concatenate([gram[i * BLOCK:(i + 1) * BLOCK, j * BLOCK:(j + 1) * BLOCK]
                            for i in range(blocks) for j in range(i, blocks)])


def factorize(packed, real):
    blocks = -(-real // BLOCK)
    size = blocks * BLOCK
    return pl.pallas_call(
        functools.partial(factor_kernel, real),
        out_shape=(jax.ShapeDtypeStruct((real, real), F32),) * 2,
        scratch_shapes=[pltpu.VMEM((blocks, BLOCK, 2 * size), F32), pltpu.VMEM((BLOCK, 2 * BLOCK), F32)],
        compiler_params=pltpu.CompilerParams(vmem_limit_bytes=60 << 20),
        name="factor",
    )(packed)


def solve_kernel(count, spots_ref, own_ref, inverse_ref, *refs):
    pieces, (out_ref, stage, value, sems) = refs[:count], refs[count:]
    copies = [pltpu.make_async_copy(piece, stage.at[spots_ref[s]], sems.at[s]) for s, piece in enumerate(pieces)]
    for copy in copies:
        copy.start()
    _, outer, cols = out_ref.shape
    low = inverse_ref[pl.ds(pl.multiple_of(own_ref[0] * cols, 8), cols), :]
    terms = []
    for _ in range(3):
        term = low.astype(BF16)
        low = low - term.astype(F32)
        terms.append(term)
    for copy in copies:
        copy.wait()
    rows = stage.shape[1]

    def one_part(n, carry):
        data = stage[n]
        value[pl.ds(pl.multiple_of(n * rows, 8), rows), :] = sum(
            lax.dot_general(data, term, (((1,), (1,)), ((), ())), preferred_element_type=F32) for term in terms)
        return carry

    lax.fori_loop(0, count, one_part, 0)
    pairs = outer // 2
    for d in range(BOND):
        for e in range(BOND):
            for i in range(2):
                data = value[pl.ds(d * 16 + i * 8 + e, pairs, stride=BOND * 16), :]
                out_ref[d * BOND + e, pl.ds(i, pairs, stride=2), :] = data


def solve(pieces, inverse, spots, own, cols):
    rows, width = pieces[0].shape
    outer = rows * len(pieces) // (BOND * 8)
    smem = pl.BlockSpec(memory_space=pltpu.SMEM)
    return pl.pallas_call(
        functools.partial(solve_kernel, len(pieces)),
        in_specs=[smem, smem, pl.BlockSpec(memory_space=pltpu.VMEM)] + [pl.BlockSpec(memory_space=pl.ANY)] * len(pieces),
        out_shape=jax.ShapeDtypeStruct((BOND * BOND, outer, cols), F32),
        scratch_shapes=[pltpu.VMEM((len(pieces), rows, width), BF16), pltpu.VMEM((rows * len(pieces), cols), F32),
                        pltpu.SemaphoreType.DMA((len(pieces),))],
        compiler_params=pltpu.CompilerParams(vmem_limit_bytes=60 << 20),
        name="solve",
    )(spots, own, inverse, *pieces)


def swap(x, mask):
    count = lax.axis_size("wide") * lax.axis_size("narrow")
    return lax.ppermute(x, ("wide", "narrow"), [(i, i ^ mask) for i in range(count)])


def bits_of(axis):
    return lax.axis_size(axis).bit_length() - 1


def gather_wide(x, after=()):
    if after:
        x = lax.optimization_barrier((x,) + tuple(after))[0]
    if lax.axis_size("wide") != 8:
        whole = lax.all_gather(x, "wide", axis=1, tiled=True)
        return [(0, 0, whole)], [whole]
    low = lax.axis_size("narrow")
    one, two, six = low, 2 * low, 6 * low
    blocks = {0: x, 1: swap(x, one), 2: swap(x, two), 6: swap(x, six)}
    blocks[3] = swap(blocks[2], one)
    blocks[4] = swap(blocks[6], two)
    blocks[7] = swap(blocks[1], six)
    blocks[5] = swap(blocks[4], one)
    return [(m, 0, blocks[m]) for m in range(8)], [blocks[3], blocks[5], blocks[7]]


def gather_narrow(x):
    blocks = [x]
    for bit in reversed(range(bits_of("narrow"))):
        blocks = blocks + [swap(b, 1 << bit) for b in blocks]
    return blocks


def narrow_masks():
    masks = [0]
    for bit in reversed(range(bits_of("narrow"))):
        masks = masks + [m | (1 << bit) for m in masks]
    return masks


def groups():
    bits = bits_of("narrow") + bits_of("wide")
    first = bits % 2
    out = [[1]] if first else []
    for b in range(first, bits, 2):
        out.append([1 << b, 2 << b])
    return out


def place_in(group, me):
    place, masks = 0, [0]
    for n, mask in enumerate(group):
        place = place + (((me // mask) % 2) << n)
        masks = masks + [m | mask for m in masks]
    return place, masks


def sum_group(x, group, me):
    place, masks = place_in(group, me)
    parts = x.reshape(len(masks), x.shape[0] // len(masks), x.shape[1])
    total = lax.dynamic_index_in_dim(parts, place, 0, False)
    for n, mask in list(enumerate(masks))[1:]:
        total = total + swap(lax.dynamic_index_in_dim(parts, place ^ n, 0, False), mask)
    return total


def join_group(x, group, me):
    place, masks = place_in(group, me)
    parts = jnp.stack([x] + [swap(x, mask) for mask in masks[1:]])
    return jnp.concatenate([lax.dynamic_index_in_dim(parts, place ^ n, 0, False) for n in range(len(masks))])


def move(left_edge, corner, right_edge, single_layer, warm_basis):
    local_rows, square, depth = left_edge.shape
    breadth = corner.shape[1]
    local_cols = right_edge.shape[2]
    narrow = lax.axis_size("narrow")
    own = lax.axis_index("narrow").astype(jnp.int32)
    me = lax.axis_index("wide").astype(jnp.int32) * narrow + own

    right, ahead = gather_wide(right_edge.transpose(1, 0, 2))
    lefts = [x.reshape(square * local_rows, depth) for x in gather_narrow(left_edge.transpose(1, 0, 2))]
    corners = gather_narrow(corner)
    half_left = half_left_of(lefts, corners, local_rows + -local_rows % OUTER)
    first, second = site_operands(single_layer)
    order = jnp.arange(shape_of(right)[0], dtype=jnp.int32)
    if len(right) > 1:
        order = order ^ (me // narrow)
    basis, _ = gather_wide(warm_basis.transpose(0, 2, 1), ahead)

    steps = half_left.shape[0] // ROWS
    cuts = [0, 3, 5, steps] if steps > 5 else [0, steps]
    enlarged = None
    for n in range(len(cuts) - 1):
        made = enlarge(half_left, right, order, first, second, cuts[n], cuts[n + 1] - cuts[n], enlarged)
        enlarged = made[0]
        if n == 0:
            right = made[1]

    half = enlarged.shape[0] // 2
    spot = lambda *masks: jnp.stack([own ^ m for m in masks])

    def summed(product):
        parts = product.reshape(2, half // 2, breadth)
        mine = lax.dynamic_index_in_dim(parts, own % 2, 0, False)
        other = swap(lax.dynamic_index_in_dim(parts, 1 - own % 2, 0, False), 1)
        return mine.astype(F32) + other.astype(F32)

    product, basis = project(enlarged, basis, order, (1 - own // 2)[None], half, breadth)
    near = summed(product).astype(BF16)
    enlarged, near = lax.optimization_barrier((enlarged, near))
    near = swap(near, 2)
    product = project(enlarged, basis, order, (own // 2)[None], half, breadth)
    rows = (summed(product[0]) + near.astype(F32)).astype(BF16)

    gram = lax.dot_general(rows, rows, (((0,), (0,)), ((), ())), preferred_element_type=F32) / (breadth * square)
    gram = packed_blocks(gram)
    for group in groups():
        gram = sum_group(gram, group, me)
    for group in reversed(groups()):
        gram = join_group(gram, group, me)
    rows, gram = lax.optimization_barrier((rows, gram))
    pieces = gather_narrow(rows)
    upper, inverse = factorize(gram, breadth)
    new_basis = solve(pieces, inverse, spot(*narrow_masks()), own[None], local_cols)
    return new_basis.transpose(1, 0, 2)[:local_rows], upper


def solution(mesh):
    placed = (
        P("wide", None, "narrow"),
        P("narrow", None),
        P("wide", None, "narrow"),
        P(),
        P(None, "narrow", "wide"),
    )
    return jax.shard_map(
        move,
        mesh=mesh,
        in_specs=placed,
        out_specs=(P("wide", None, "narrow"), P()),
        check_vma=False,
    )
```

```python
import functools
import jax
import jax.numpy as jnp
from jax import lax
from jax.experimental import pallas as pl
from jax.experimental.pallas import tpu as pltpu
from jax.sharding import PartitionSpec as P


BOND = 7
LANES = 128
BLOCK = 128
PANEL = 8
GROUP = 8
OUTER = 8
ROWS = OUTER * 64
TIGHT = OUTER * BOND * 8
SPLIT = 7
F32 = jnp.float32
BF16 = jnp.bfloat16
HIGHEST = lax.Precision.HIGHEST


def site_operands(single_layer):
    phys = single_layer.shape[0]
    layer = single_layer.reshape(phys, BOND, BOND, BOND, BOND)
    half = 4
    padded = jnp.pad(layer, ((0, 0), (0, 1), (0, 0), (0, 0), (0, 0)))
    eye = jnp.eye(half, dtype=layer.dtype)
    first = padded.transpose(3, 4, 0, 2, 1)[:, :, :, None, :, None, :] * eye[None, None, None, :, None, :, None]
    first = first.reshape(BOND * BOND * phys * half, BOND * half * 8)
    split = padded.reshape(phys, 2, half, BOND, BOND, BOND)
    second = jnp.pad(split.transpose(5, 4, 3, 1, 0, 2), ((0, 0), (0, 1), (0, 0), (0, 0), (0, 0), (0, 0)))
    return first, second.reshape(BOND * 8, BOND * 2 * phys * half)


def assemble(layout, order_ref, pieces, stage, target, sems):
    copies = [pltpu.make_async_copy(piece, stage.at[block, pl.ds(begin, size)], sems.at[s])
              for s, ((block, begin, size), piece) in enumerate(zip(layout, pieces))]
    for copy in copies:
        copy.start()
    target[...] = jnp.zeros_like(target)
    for copy in copies:
        copy.wait()
    count, square, depth, breadth = stage.shape

    def fill(q, carry):
        lane = pl.ds(pl.multiple_of(q * LANES, LANES), breadth)
        if count == 1:
            target[:, lane] = stage[0, q]
        for pair in range(count // 2):
            joined = jnp.concatenate(
                [stage[order_ref[2 * pair + k], q].astype(F32) for k in range(2)], axis=0)
            target[pl.ds(pair * 2 * depth, 2 * depth), lane] = joined.astype(BF16)
        return carry

    lax.fori_loop(0, square, fill, 0)


def half_left_kernel(parts_of, *refs):
    left_refs, corner_refs = refs[:parts_of], refs[parts_of:2 * parts_of]
    out_ref, total, spread = refs[2 * parts_of:]
    value = jnp.dot(left_refs[0][...], corner_refs[0][...], preferred_element_type=F32)
    for n in range(1, parts_of):
        value += jnp.dot(left_refs[n][...], corner_refs[n][...], preferred_element_type=F32)
    outer = total.shape[0] // (BOND * BOND)
    spread[...] = jnp.zeros_like(spread)
    width = value.shape[1]
    total[:, :width] = value

    def place(u, v):
        begin = (u * BOND + v) * outer
        if outer % 8 == 0:
            begin = pl.multiple_of(begin, 8)
        for c in range(spread.shape[0]):
            data = total[pl.ds(begin, outer), c * LANES:(c + 1) * LANES]
            spread[c, pl.ds(v * 8 + u, outer, stride=BOND * 8), :] = data

    if outer % 8 == 0:
        lax.fori_loop(0, BOND * BOND, lambda p, carry: (place(p // BOND, p % BOND), carry)[1], 0)
    else:
        for p in range(BOND * BOND):
            place(p // BOND, p % BOND)
    for c in range(spread.shape[0]):
        count = min(LANES, width - c * LANES)
        out_ref[:, c * LANES:c * LANES + count] = spread[c, :, :count].astype(BF16)


def half_left_of(lefts, corners, outer):
    width = corners[0].shape[1]
    return pl.pallas_call(
        functools.partial(half_left_kernel, len(lefts)),
        out_shape=jax.ShapeDtypeStruct((outer * BOND * 8, width), BF16),
        scratch_shapes=[pltpu.VMEM((lefts[0].shape[0], -(-width // LANES) * LANES), F32),
                        pltpu.VMEM((-(-width // LANES), outer * BOND * 8, LANES), F32)],
        compiler_params=pltpu.CompilerParams(vmem_limit_bytes=60 << 20),
        name="half_left",
    )(*lefts, *corners)


def enlarge_kernel(layout, order_ref, half_ref, first_ref, second_ref, *rest):
    count = len(layout)
    if count:
        pieces, (out_ref, right_all, stage, strip, ket, sems) = rest[:count], rest[count:]

        @pl.when(pl.program_id(0) == 0)
        def _():
            assemble(layout, order_ref, pieces, stage, right_all, sems)
    else:
        right_all, _, out_ref, strip, ket = rest
    rows = strip.shape[1]
    square = BOND * BOND
    span = BOND * LANES
    half_left = half_ref[...]
    for l in range(BOND):
        value = jnp.dot(half_left, right_all[:, l * span:(l + 1) * span], preferred_element_type=F32)
        value = jnp.concatenate([value.reshape(OUTER, BOND * 8, span), jnp.zeros((OUTER, 8, span), F32)], axis=1)
        strip[l] = value.astype(BF16).reshape(rows, span)

    def one_pair(pair, carry):
        for i in range(2):
            parts = []
            for g in range(2):
                at = pl.ds(pl.multiple_of((pair * 2 + i) * 64 + g * 32, 32), 32)
                data = strip[:, at, :].reshape(BOND * 32, span)
                part = jnp.dot(first_ref[...], data, preferred_element_type=F32)
                parts.append(part.reshape(square, 8, span))
            ket[i] = jnp.concatenate(parts, axis=1).astype(BF16)
        for d in range(BOND):
            rows_of = []
            for lp in range(BOND):
                rows_of.append(jnp.concatenate(
                    [ket[i, d * BOND + r, :, lp * LANES:(lp + 1) * LANES] for r in range(BOND) for i in range(2)],
                    axis=1))
            data = jnp.concatenate(rows_of, axis=0)
            value = jnp.dot(second_ref[...], data, preferred_element_type=F32)
            at = pl.ds(pl.multiple_of((pair * BOND + d) * 16, 16), 16)
            for r in range(BOND):
                two = [value[:, (r * 2 + i) * LANES:(r * 2 + i + 1) * LANES].reshape(BOND, 8, LANES)
                       for i in range(2)]
                both = jnp.concatenate(two, axis=1).astype(BF16)
                for rp in range(BOND):
                    out_ref[at, (r * BOND + rp) * LANES:(r * BOND + rp + 1) * LANES] = both[rp]
        return carry

    lax.fori_loop(0, rows // 128, one_pair, 0)


def whole_block(a):
    return pl.BlockSpec(a.shape, lambda s: (0,) * a.ndim, pipeline_mode=pl.Buffered(1))


def shape_of(pieces):
    blocks = 1 + max(block for block, _, _ in pieces)
    square = sum(piece.shape[0] for block, _, piece in pieces if block == 0)
    return (blocks, square) + pieces[0][2].shape[1:]


def layout_of(pieces):
    return tuple((block, begin, piece.shape[0]) for block, begin, piece in pieces)


def enlarge(half_left, right, order, first, second, begin, steps, before=None):
    total, depth = half_left.shape
    pieces = right if isinstance(right, list) else None
    square = BOND * BOND
    lanes = square * LANES
    out_rows = ROWS // 128 * BOND * 16
    in_specs = [pl.BlockSpec(memory_space=pltpu.SMEM), pl.BlockSpec((TIGHT, depth), lambda s: (s + begin, 0)),
                whole_block(first), whole_block(second)]
    out_specs = [pl.BlockSpec((out_rows, lanes), lambda s: (s + begin, 0))]
    out_shape = [jax.ShapeDtypeStruct((total // TIGHT * out_rows, lanes), BF16)]
    scratch = [pltpu.VMEM((BOND, ROWS, BOND * LANES), BF16), pltpu.VMEM((2, square, 16, BOND * LANES), BF16)]
    if pieces:
        shape = shape_of(pieces)
        width = shape[0] * shape[2]
        in_specs += [pl.BlockSpec(memory_space=pl.ANY)] * len(pieces)
        out_specs.append(pl.BlockSpec((width, lanes), lambda s: (0, 0), pipeline_mode=pl.Buffered(1)))
        out_shape.append(jax.ShapeDtypeStruct((width, lanes), BF16))
        scratch = [pltpu.VMEM(shape, BF16)] + scratch
        scratch.append(pltpu.SemaphoreType.DMA((len(pieces),)))
    else:
        in_specs += [whole_block(right), pl.BlockSpec(memory_space=pl.ANY)]
    flops = 2 * steps * ROWS * lanes * 1024
    return pl.pallas_call(
        functools.partial(enlarge_kernel, layout_of(pieces) if pieces else ()),
        grid=(steps,),
        in_specs=in_specs,
        out_specs=out_specs,
        out_shape=out_shape,
        scratch_shapes=scratch,
        compiler_params=pltpu.CompilerParams(dimension_semantics=("arbitrary",), vmem_limit_bytes=60 << 20),
        cost_estimate=pl.CostEstimate(flops=flops, transcendentals=0, bytes_accessed=steps * out_rows * lanes * 2),
        input_output_aliases={} if pieces else {len(in_specs) - 1: 0},
        name="enlarge",
    )(order, half_left, first, second, *([p for _, _, p in pieces] if pieces else [right, before]))


def project_kernel(layout, order_ref, spot_ref, rows_ref, *refs):
    count = len(layout)
    if count:
        pieces, (out_ref, basis_all, stage, sems) = refs[:count], refs[count:]

        @pl.when(pl.program_id(0) == 0)
        def _():
            assemble(layout, order_ref, pieces, stage, basis_all, sems)
    else:
        basis_all, out_ref = refs
    out_ref[...] = lax.dot_general(rows_ref[...], basis_all[...], (((1,), (1,)), ((), ())),
                                   preferred_element_type=F32).astype(out_ref.dtype)


def project(enlarged, basis, order, spot, rows, width):
    lanes = enlarged.shape[1]
    pieces = basis if isinstance(basis, list) else None
    once = rows // SPLIT
    full = lambda shape: pl.BlockSpec(shape, lambda s, order, spot: (0,) * len(shape), pipeline_mode=pl.Buffered(1))
    in_specs = [pl.BlockSpec((once, lanes), lambda s, order, spot: (spot[0] * SPLIT + s, 0))]
    out_specs = [pl.BlockSpec((once, width), lambda s, order, spot: (s, 0))]
    out_shape = [jax.ShapeDtypeStruct((rows, width), BF16)]
    scratch = []
    if pieces:
        in_specs += [pl.BlockSpec(memory_space=pl.ANY)] * len(pieces)
        out_specs.append(full((width, lanes)))
        out_shape.append(jax.ShapeDtypeStruct((width, lanes), BF16))
        scratch += [pltpu.VMEM(shape_of(pieces), BF16), pltpu.SemaphoreType.DMA((len(pieces),))]
    else:
        in_specs.append(full(basis.shape))
    return pl.pallas_call(
        functools.partial(project_kernel, layout_of(pieces) if pieces else ()),
        grid_spec=pltpu.PrefetchScalarGridSpec(
            num_scalar_prefetch=2, grid=(SPLIT,), in_specs=in_specs, out_specs=out_specs, scratch_shapes=scratch),
        out_shape=out_shape,
        compiler_params=pltpu.CompilerParams(dimension_semantics=("arbitrary",), vmem_limit_bytes=60 << 20),
        cost_estimate=pl.CostEstimate(flops=2 * rows * width * lanes, transcendentals=0,
                                      bytes_accessed=2 * rows * lanes),
        name="project",
    )(order, spot, enlarged, *([p for _, _, p in pieces] if pieces else [basis]))


def factor_kernel(real, gram_ref, upper_ref, inverse_ref, work, cell):
    blocks = work.shape[0]
    size = blocks * BLOCK
    lane = lax.broadcasted_iota(jnp.int32, (BLOCK, size), 1)
    row = lax.broadcasted_iota(jnp.int32, (BLOCK, size), 0)
    place = 0
    for k in range(blocks):
        unit = (lane == row + k * BLOCK).astype(F32)
        work[k, :, :size] = jnp.where(lane >= real, unit, 0.0)
        work[k, :, size:] = unit
        for j in range(k, blocks):
            at = slice(j * BLOCK, (j + 1) * BLOCK)
            work[k, :, at] = work[k, :, at] + gram_ref[place * BLOCK:(place + 1) * BLOCK, :]
            place += 1
    sub = lax.broadcasted_iota(jnp.int32, (PANEL, BLOCK), 0)
    lane8 = lax.broadcasted_iota(jnp.int32, (PANEL, BLOCK), 1)
    panels = BLOCK // PANEL

    def block_step(k, carry):
        here = pl.ds(pl.multiple_of(k * BLOCK, BLOCK), BLOCK)
        cell[:, :BLOCK] = work[k, :, here]
        row_b = lax.broadcasted_iota(jnp.int32, (BLOCK, BLOCK), 0)
        lane_b = lax.broadcasted_iota(jnp.int32, (BLOCK, BLOCK), 1)
        cell[:, BLOCK:] = (row_b == lane_b).astype(F32)

        def one_panel(p):
            base = p * PANEL
            left = cell[base:base + PANEL, :BLOCK]
            right = cell[base:base + PANEL, BLOCK:]
            spread = [jnp.broadcast_to(left[:, base + t:base + t + 1], (PANEL, BLOCK)) for t in range(PANEL)]
            scale = jnp.zeros((PANEL, BLOCK), F32)
            for t in range(PANEL):
                inv = 1.0 / jnp.broadcast_to(spread[t][t:t + 1, :], (PANEL, BLOCK))
                factor = jnp.where(sub > t, spread[t] * inv, 0.0)
                scale = jnp.where(sub == t, inv, scale)
                for later in range(t + 1, PANEL):
                    spread[later] = spread[later] - factor * jnp.broadcast_to(
                        spread[later][t:t + 1, :], (PANEL, BLOCK))
                left = left - factor * jnp.broadcast_to(left[t:t + 1, :], (PANEL, BLOCK))
                right = right - factor * jnp.broadcast_to(right[t:t + 1, :], (PANEL, BLOCK))
            weights = jnp.transpose(left * scale)
            for g in range(p + 1, (p // GROUP + 1) * GROUP):
                at = slice(g * PANEL, (g + 1) * PANEL)
                a, b = cell[at, :BLOCK], cell[at, BLOCK:]
                for t in range(PANEL):
                    w = jnp.broadcast_to(weights[at, t:t + 1], (PANEL, BLOCK))
                    a = a - w * jnp.broadcast_to(left[t:t + 1, :], (PANEL, BLOCK))
                    b = b - w * jnp.broadcast_to(right[t:t + 1, :], (PANEL, BLOCK))
                cell[at, :BLOCK] = a
                cell[at, BLOCK:] = b
            root = jnp.sqrt(scale)
            cell[base:base + PANEL, :BLOCK] = left * root
            cell[base:base + PANEL, BLOCK:] = right * root
            end = base + PANEL
            if end % (GROUP * PANEL) == 0 and end < BLOCK:
                done = cell[end - GROUP * PANEL:end, :]
                change = lax.dot_general(done[:, :BLOCK], done, (((0,), (0,)), ((), ())),
                                         precision=HIGHEST, preferred_element_type=F32)
                cell[end:, :] = cell[end:, :] - change[end:, :]

        sure = (real - (blocks - 1) * BLOCK + PANEL - 1) // PANEL
        for p in range(sure):
            one_panel(p)

        @pl.when(k < blocks - 1)
        def _():
            for p in range(sure, panels):
                one_panel(p)

        window = pl.ds(pl.multiple_of(k * BLOCK, BLOCK), size + BLOCK)
        mine = jnp.dot(cell[:, BLOCK:], work[k, :, window], precision=HIGHEST, preferred_element_type=F32)
        work[k, :, window] = mine

        @pl.when(k < blocks - 1)
        def _():
            change = lax.dot_general(mine[:, BLOCK:size], mine, (((0,), (0,)), ((), ())),
                                     precision=HIGHEST, preferred_element_type=F32)
            for n in range(blocks - 1):
                @pl.when(k + 1 + n < blocks)
                def _():
                    work[k + 1 + n, :, window] = work[k + 1 + n, :, window] - change[n * BLOCK:(n + 1) * BLOCK]

        return carry

    lax.fori_loop(0, blocks, block_step, 0)
    for k in range(blocks):
        count = min(BLOCK, real - k * BLOCK)
        at = slice(k * BLOCK, k * BLOCK + count)
        upper = jnp.where(lane >= row + k * BLOCK, work[k, :, :size], 0.0)
        upper_ref[at, :] = upper[:count, :real]
        inverse_ref[at, :] = work[k, :count, size:size + real]


def packed_blocks(gram):
    real = gram.shape[0]
    spare = -real % BLOCK
    gram = jnp.pad(gram, ((0, spare), (0, spare)))
    blocks = gram.shape[0] // BLOCK
    return jnp.concatenate([gram[i * BLOCK:(i + 1) * BLOCK, j * BLOCK:(j + 1) * BLOCK]
                            for i in range(blocks) for j in range(i, blocks)])


def factorize(packed, real):
    blocks = -(-real // BLOCK)
    size = blocks * BLOCK
    return pl.pallas_call(
        functools.partial(factor_kernel, real),
        out_shape=(jax.ShapeDtypeStruct((real, real), F32),) * 2,
        scratch_shapes=[pltpu.VMEM((blocks, BLOCK, 2 * size), F32), pltpu.VMEM((BLOCK, 2 * BLOCK), F32)],
        compiler_params=pltpu.CompilerParams(vmem_limit_bytes=60 << 20),
        name="factor",
    )(packed)


def solve_kernel(count, spots_ref, own_ref, inverse_ref, *refs):
    pieces, (out_ref, stage, value, sems) = refs[:count], refs[count:]
    copies = [pltpu.make_async_copy(piece, stage.at[spots_ref[s]], sems.at[s]) for s, piece in enumerate(pieces)]
    for copy in copies:
        copy.start()
    _, outer, cols = out_ref.shape
    low = inverse_ref[pl.ds(pl.multiple_of(own_ref[0] * cols, 8), cols), :]
    terms = []
    for _ in range(2):
        term = low.astype(BF16)
        low = low - term.astype(F32)
        terms.append(term)
    for copy in copies:
        copy.wait()
    rows = stage.shape[1]

    def one_part(n, carry):
        data = stage[n]
        value[pl.ds(pl.multiple_of(n * rows, 8), rows), :] = sum(
            lax.dot_general(data, term, (((1,), (1,)), ((), ())), preferred_element_type=F32) for term in terms)
        return carry

    lax.fori_loop(0, count, one_part, 0)
    pairs = outer // 2
    for d in range(BOND):
        for e in range(BOND):
            for i in range(2):
                data = value[pl.ds(d * 16 + i * 8 + e, pairs, stride=BOND * 16), :]
                out_ref[d * BOND + e, pl.ds(i, pairs, stride=2), :] = data


def solve(pieces, inverse, spots, own, cols):
    rows, width = pieces[0].shape
    outer = rows * len(pieces) // (BOND * 8)
    smem = pl.BlockSpec(memory_space=pltpu.SMEM)
    return pl.pallas_call(
        functools.partial(solve_kernel, len(pieces)),
        in_specs=[smem, smem, pl.BlockSpec(memory_space=pltpu.VMEM)] + [pl.BlockSpec(memory_space=pl.ANY)] * len(pieces),
        out_shape=jax.ShapeDtypeStruct((BOND * BOND, outer, cols), F32),
        scratch_shapes=[pltpu.VMEM((len(pieces), rows, width), BF16), pltpu.VMEM((rows * len(pieces), cols), F32),
                        pltpu.SemaphoreType.DMA((len(pieces),))],
        compiler_params=pltpu.CompilerParams(vmem_limit_bytes=60 << 20),
        name="solve",
    )(spots, own, inverse, *pieces)


def swap(x, mask):
    count = lax.axis_size("wide") * lax.axis_size("narrow")
    return lax.ppermute(x, ("wide", "narrow"), [(i, i ^ mask) for i in range(count)])


def bits_of(axis):
    return lax.axis_size(axis).bit_length() - 1


def gather_wide(x, after=()):
    if after:
        x = lax.optimization_barrier((x,) + tuple(after))[0]
    if lax.axis_size("wide") != 8:
        whole = lax.all_gather(x, "wide", axis=1, tiled=True)
        return [(0, 0, whole)], [whole]
    low = lax.axis_size("narrow")
    one, two, six = low, 2 * low, 6 * low
    blocks = {0: x, 1: swap(x, one), 2: swap(x, two), 6: swap(x, six)}
    blocks[3] = swap(blocks[2], one)
    blocks[4] = swap(blocks[6], two)
    blocks[7] = swap(blocks[1], six)
    blocks[5] = swap(blocks[4], one)
    return [(m, 0, blocks[m]) for m in range(8)], [blocks[3], blocks[5], blocks[7]]


def gather_narrow(x):
    blocks = [x]
    for bit in reversed(range(bits_of("narrow"))):
        blocks = blocks + [swap(b, 1 << bit) for b in blocks]
    return blocks


def narrow_masks():
    masks = [0]
    for bit in reversed(range(bits_of("narrow"))):
        masks = masks + [m | (1 << bit) for m in masks]
    return masks


def groups():
    bits = bits_of("narrow") + bits_of("wide")
    first = bits % 2
    out = [[1]] if first else []
    for b in range(first, bits, 2):
        out.append([1 << b, 2 << b])
    return out


def place_in(group, me):
    place, masks = 0, [0]
    for n, mask in enumerate(group):
        place = place + (((me // mask) % 2) << n)
        masks = masks + [m | mask for m in masks]
    return place, masks


def sum_group(x, group, me):
    place, masks = place_in(group, me)
    parts = x.reshape(len(masks), x.shape[0] // len(masks), x.shape[1])
    total = lax.dynamic_index_in_dim(parts, place, 0, False)
    for n, mask in list(enumerate(masks))[1:]:
        total = total + swap(lax.dynamic_index_in_dim(parts, place ^ n, 0, False), mask)
    return total


def join_group(x, group, me):
    place, masks = place_in(group, me)
    parts = jnp.stack([x] + [swap(x, mask) for mask in masks[1:]])
    return jnp.concatenate([lax.dynamic_index_in_dim(parts, place ^ n, 0, False) for n in range(len(masks))])


def move(left_edge, corner, right_edge, single_layer, warm_basis):
    local_rows, square, depth = left_edge.shape
    breadth = corner.shape[1]
    local_cols = right_edge.shape[2]
    narrow = lax.axis_size("narrow")
    own = lax.axis_index("narrow").astype(jnp.int32)
    me = lax.axis_index("wide").astype(jnp.int32) * narrow + own

    right, ahead = gather_wide(right_edge.transpose(1, 0, 2))
    lefts = [x.reshape(square * local_rows, depth) for x in gather_narrow(left_edge.transpose(1, 0, 2))]
    corners = gather_narrow(corner)
    half_left = half_left_of(lefts, corners, local_rows + -local_rows % OUTER)
    first, second = site_operands(single_layer)
    order = jnp.arange(shape_of(right)[0], dtype=jnp.int32)
    if len(right) > 1:
        order = order ^ (me // narrow)
    basis, _ = gather_wide(warm_basis.transpose(0, 2, 1), ahead)

    steps = half_left.shape[0] // TIGHT
    cuts = [0, 3, 5, steps] if steps > 5 else [0, steps]
    enlarged = None
    for n in range(len(cuts) - 1):
        made = enlarge(half_left, right, order, first, second, cuts[n], cuts[n + 1] - cuts[n], enlarged)
        enlarged = made[0]
        if n == 0:
            right = made[1]

    half = enlarged.shape[0] // 2
    spot = lambda *masks: jnp.stack([own ^ m for m in masks])

    def summed(product):
        parts = product.reshape(2, half // 2, breadth)
        mine = lax.dynamic_index_in_dim(parts, own % 2, 0, False)
        other = swap(lax.dynamic_index_in_dim(parts, 1 - own % 2, 0, False), 1)
        return mine.astype(F32) + other.astype(F32)

    product, basis = project(enlarged, basis, order, (1 - own // 2)[None], half, breadth)
    near = summed(product).astype(BF16)
    enlarged, near = lax.optimization_barrier((enlarged, near))
    near = swap(near, 2)
    product = project(enlarged, basis, order, (own // 2)[None], half, breadth)
    rows = (summed(product[0]) + near.astype(F32)).astype(BF16)

    gram = lax.dot_general(rows, rows, (((0,), (0,)), ((), ())), preferred_element_type=F32) / (breadth * square)
    gram = packed_blocks(gram)
    for group in groups():
        gram = sum_group(gram, group, me)
    for group in reversed(groups()):
        gram = join_group(gram, group, me)
    rows, gram = lax.optimization_barrier((rows, gram))
    pieces = gather_narrow(rows)
    upper, inverse = factorize(gram, breadth)
    new_basis = solve(pieces, inverse, spot(*narrow_masks()), own[None], local_cols)
    return new_basis.transpose(1, 0, 2)[:local_rows], upper


def solution(mesh):
    placed = (
        P("wide", None, "narrow"),
        P("narrow", None),
        P("wide", None, "narrow"),
        P(),
        P(None, "narrow", "wide"),
    )
    return jax.shard_map(
        move,
        mesh=mesh,
        in_specs=placed,
        out_specs=(P("wide", None, "narrow"), P()),
        check_vma=False,
    )
```

```python
import functools
import jax
import jax.numpy as jnp
from jax import lax
from jax.experimental import pallas as pl
from jax.experimental.pallas import tpu as pltpu
from jax.sharding import PartitionSpec as P


BOND = 7
LANES = 128
BLOCK = 128
PANEL = 8
GROUP = 8
OUTER = 8
ROWS = OUTER * 64
TIGHT = OUTER * BOND * 8
SPLIT = 7
F32 = jnp.float32
BF16 = jnp.bfloat16
HIGHEST = lax.Precision.HIGHEST


def site_operands(single_layer):
    phys = single_layer.shape[0]
    layer = single_layer.reshape(phys, BOND, BOND, BOND, BOND)
    half = 4
    padded = jnp.pad(layer, ((0, 0), (0, 1), (0, 0), (0, 0), (0, 0)))
    eye = jnp.eye(half, dtype=layer.dtype)
    first = padded.transpose(3, 4, 0, 2, 1)[:, :, :, None, :, None, :] * eye[None, None, None, :, None, :, None]
    first = first.reshape(BOND * BOND * phys * half, BOND * half * 8)
    split = padded.reshape(phys, 2, half, BOND, BOND, BOND)
    second = jnp.pad(split.transpose(5, 4, 3, 1, 0, 2), ((0, 0), (0, 1), (0, 0), (0, 0), (0, 0), (0, 0)))
    return first, second.reshape(BOND * 8, BOND * 2 * phys * half)


def assemble(layout, order_ref, pieces, stage, target, sems):
    copies = [pltpu.make_async_copy(piece, stage.at[block, pl.ds(begin, size)], sems.at[s])
              for s, ((block, begin, size), piece) in enumerate(zip(layout, pieces))]
    for copy in copies:
        copy.start()
    target[...] = jnp.zeros_like(target)
    for copy in copies:
        copy.wait()
    count, square, depth, breadth = stage.shape

    def fill(q, carry):
        lane = pl.ds(pl.multiple_of(q * LANES, LANES), breadth)
        if count == 1:
            target[:, lane] = stage[0, q]
        for pair in range(count // 2):
            joined = jnp.concatenate(
                [stage[order_ref[2 * pair + k], q].astype(F32) for k in range(2)], axis=0)
            target[pl.ds(pair * 2 * depth, 2 * depth), lane] = joined.astype(BF16)
        return carry

    lax.fori_loop(0, square, fill, 0, unroll=BOND)


def half_left_kernel(parts_of, *refs):
    left_refs, corner_refs = refs[:parts_of], refs[parts_of:2 * parts_of]
    out_ref, total, spread = refs[2 * parts_of:]
    value = jnp.dot(left_refs[0][...], corner_refs[0][...], preferred_element_type=F32)
    for n in range(1, parts_of):
        value += jnp.dot(left_refs[n][...], corner_refs[n][...], preferred_element_type=F32)
    outer = total.shape[0] // (BOND * BOND)
    spread[...] = jnp.zeros_like(spread)
    width = value.shape[1]
    total[:, :width] = value

    def place(u, v):
        begin = (u * BOND + v) * outer
        if outer % 8 == 0:
            begin = pl.multiple_of(begin, 8)
        for c in range(spread.shape[0]):
            data = total[pl.ds(begin, outer), c * LANES:(c + 1) * LANES]
            spread[c, pl.ds(v * 8 + u, outer, stride=BOND * 8), :] = data

    if outer % 8 == 0:
        lax.fori_loop(0, BOND * BOND, lambda p, carry: (place(p // BOND, p % BOND), carry)[1], 0)
    else:
        for p in range(BOND * BOND):
            place(p // BOND, p % BOND)
    for c in range(spread.shape[0]):
        count = min(LANES, width - c * LANES)
        out_ref[:, c * LANES:c * LANES + count] = spread[c, :, :count].astype(BF16)


def half_left_of(lefts, corners, outer):
    width = corners[0].shape[1]
    return pl.pallas_call(
        functools.partial(half_left_kernel, len(lefts)),
        out_shape=jax.ShapeDtypeStruct((outer * BOND * 8, width), BF16),
        scratch_shapes=[pltpu.VMEM((lefts[0].shape[0], -(-width // LANES) * LANES), F32),
                        pltpu.VMEM((-(-width // LANES), outer * BOND * 8, LANES), F32)],
        compiler_params=pltpu.CompilerParams(vmem_limit_bytes=60 << 20),
        name="half_left",
    )(*lefts, *corners)


def enlarge_kernel(layout, order_ref, half_ref, first_ref, second_ref, *rest):
    count = len(layout)
    if count:
        pieces, (out_ref, right_all, stage, strip, ket, sems) = rest[:count], rest[count:]

        @pl.when(pl.program_id(0) == 0)
        def _():
            assemble(layout, order_ref, pieces, stage, right_all, sems)
    else:
        right_all, _, out_ref, strip, ket = rest
    rows = strip.shape[1]
    square = BOND * BOND
    span = BOND * LANES
    half_left = half_ref[...]
    for l in range(BOND):
        value = jnp.dot(half_left, right_all[:, l * span:(l + 1) * span], preferred_element_type=F32)
        value = jnp.concatenate([value.reshape(OUTER, BOND * 8, span), jnp.zeros((OUTER, 8, span), F32)], axis=1)
        strip[l] = value.astype(BF16).reshape(rows, span)

    def one_pair(pair, carry):
        for i in range(2):
            parts = []
            for g in range(2):
                at = pl.ds(pl.multiple_of((pair * 2 + i) * 64 + g * 32, 32), 32)
                data = strip[:, at, :].reshape(BOND * 32, span)
                part = jnp.dot(first_ref[...], data, preferred_element_type=F32)
                parts.append(part.reshape(square, 8, span))
            ket[i] = jnp.concatenate(parts, axis=1).astype(BF16)
        for d in range(BOND):
            rows_of = []
            for lp in range(BOND):
                rows_of.append(jnp.concatenate(
                    [ket[i, d * BOND + r, :, lp * LANES:(lp + 1) * LANES] for r in range(BOND) for i in range(2)],
                    axis=1))
            data = jnp.concatenate(rows_of, axis=0)
            value = jnp.dot(second_ref[...], data, preferred_element_type=F32)
            at = pl.ds(pl.multiple_of((pair * BOND + d) * 16, 16), 16)
            for r in range(BOND):
                two = [value[:, (r * 2 + i) * LANES:(r * 2 + i + 1) * LANES].reshape(BOND, 8, LANES)
                       for i in range(2)]
                both = jnp.concatenate(two, axis=1).astype(BF16)
                for rp in range(BOND):
                    out_ref[at, (r * BOND + rp) * LANES:(r * BOND + rp + 1) * LANES] = both[rp]
        return carry

    lax.fori_loop(0, rows // 128, one_pair, 0)


def whole_block(a):
    return pl.BlockSpec(a.shape, lambda s: (0,) * a.ndim, pipeline_mode=pl.Buffered(1))


def shape_of(pieces):
    blocks = 1 + max(block for block, _, _ in pieces)
    square = sum(piece.shape[0] for block, _, piece in pieces if block == 0)
    return (blocks, square) + pieces[0][2].shape[1:]


def layout_of(pieces):
    return tuple((block, begin, piece.shape[0]) for block, begin, piece in pieces)


def enlarge(half_left, right, order, first, second, begin, steps, before=None):
    total, depth = half_left.shape
    pieces = right if isinstance(right, list) else None
    square = BOND * BOND
    lanes = square * LANES
    out_rows = ROWS // 128 * BOND * 16
    in_specs = [pl.BlockSpec(memory_space=pltpu.SMEM), pl.BlockSpec((TIGHT, depth), lambda s: (s + begin, 0)),
                whole_block(first), whole_block(second)]
    out_specs = [pl.BlockSpec((out_rows, lanes), lambda s: (s + begin, 0))]
    out_shape = [jax.ShapeDtypeStruct((total // TIGHT * out_rows, lanes), BF16)]
    scratch = [pltpu.VMEM((BOND, ROWS, BOND * LANES), BF16), pltpu.VMEM((2, square, 16, BOND * LANES), BF16)]
    if pieces:
        shape = shape_of(pieces)
        width = shape[0] * shape[2]
        in_specs += [pl.BlockSpec(memory_space=pl.ANY)] * len(pieces)
        out_specs.append(pl.BlockSpec((width, lanes), lambda s: (0, 0), pipeline_mode=pl.Buffered(1)))
        out_shape.append(jax.ShapeDtypeStruct((width, lanes), BF16))
        scratch = [pltpu.VMEM(shape, BF16)] + scratch
        scratch.append(pltpu.SemaphoreType.DMA((len(pieces),)))
    else:
        in_specs += [whole_block(right), pl.BlockSpec(memory_space=pl.ANY)]
    flops = 2 * steps * ROWS * lanes * 1024
    return pl.pallas_call(
        functools.partial(enlarge_kernel, layout_of(pieces) if pieces else ()),
        grid=(steps,),
        in_specs=in_specs,
        out_specs=out_specs,
        out_shape=out_shape,
        scratch_shapes=scratch,
        compiler_params=pltpu.CompilerParams(dimension_semantics=("arbitrary",), vmem_limit_bytes=60 << 20),
        cost_estimate=pl.CostEstimate(flops=flops, transcendentals=0, bytes_accessed=steps * out_rows * lanes * 2),
        input_output_aliases={} if pieces else {len(in_specs) - 1: 0},
        name="enlarge",
    )(order, half_left, first, second, *([p for _, _, p in pieces] if pieces else [right, before]))


def project_kernel(layout, order_ref, spot_ref, rows_ref, *refs):
    count = len(layout)
    if count:
        pieces, (mine_ref, other_ref, basis_all, stage, sems) = refs[:count], refs[count:]

        @pl.when(pl.program_id(0) == 0)
        def _():
            assemble(layout, order_ref, pieces, stage, basis_all, sems)
    else:
        basis_all, mine_ref, other_ref = refs
    value = lax.dot_general(rows_ref[...], basis_all[...], (((1,), (1,)), ((), ())),
                            preferred_element_type=F32).astype(BF16)
    chunk = value.shape[0] // 2
    for upper, (low_ref, high_ref) in enumerate(((mine_ref, other_ref), (other_ref, mine_ref))):
        @pl.when(spot_ref[1] == upper)
        def _():
            low_ref[...] = value[:chunk]
            high_ref[...] = value[chunk:]


def project(enlarged, basis, order, spot, rows, width):
    lanes = enlarged.shape[1]
    pieces = basis if isinstance(basis, list) else None
    once = rows // SPLIT
    full = lambda shape: pl.BlockSpec(shape, lambda s, order, spot: (0,) * len(shape), pipeline_mode=pl.Buffered(1))
    in_specs = [pl.BlockSpec((once, lanes), lambda s, order, spot: (spot[0] * SPLIT + s, 0))]
    out_specs = [pl.BlockSpec((once // 2, width), lambda s, order, spot: (s, 0))] * 2
    out_shape = [jax.ShapeDtypeStruct((rows // 2, width), BF16)] * 2
    scratch = []
    if pieces:
        in_specs += [pl.BlockSpec(memory_space=pl.ANY)] * len(pieces)
        out_specs.append(full((width, lanes)))
        out_shape.append(jax.ShapeDtypeStruct((width, lanes), BF16))
        scratch += [pltpu.VMEM(shape_of(pieces), BF16), pltpu.SemaphoreType.DMA((len(pieces),))]
    else:
        in_specs.append(full(basis.shape))
    return pl.pallas_call(
        functools.partial(project_kernel, layout_of(pieces) if pieces else ()),
        grid_spec=pltpu.PrefetchScalarGridSpec(
            num_scalar_prefetch=2, grid=(SPLIT,), in_specs=in_specs, out_specs=out_specs, scratch_shapes=scratch),
        out_shape=out_shape,
        compiler_params=pltpu.CompilerParams(dimension_semantics=("arbitrary",), vmem_limit_bytes=60 << 20),
        cost_estimate=pl.CostEstimate(flops=2 * rows * width * lanes, transcendentals=0,
                                      bytes_accessed=2 * rows * lanes),
        name="project",
    )(order, spot, enlarged, *([p for _, _, p in pieces] if pieces else [basis]))


def factor_kernel(real, gram_ref, upper_ref, inverse_ref, work, cell):
    blocks = work.shape[0]
    size = blocks * BLOCK
    lane = lax.broadcasted_iota(jnp.int32, (BLOCK, size), 1)
    row = lax.broadcasted_iota(jnp.int32, (BLOCK, size), 0)
    place = 0
    for k in range(blocks):
        unit = (lane == row + k * BLOCK).astype(F32)
        work[k, :, :size] = jnp.where(lane >= real, unit, 0.0)
        work[k, :, size:] = unit
        for j in range(k, blocks):
            at = slice(j * BLOCK, (j + 1) * BLOCK)
            work[k, :, at] = work[k, :, at] + gram_ref[place * BLOCK:(place + 1) * BLOCK, :]
            place += 1
    sub = lax.broadcasted_iota(jnp.int32, (PANEL, BLOCK), 0)
    lane8 = lax.broadcasted_iota(jnp.int32, (PANEL, BLOCK), 1)
    panels = BLOCK // PANEL

    def block_step(k, carry):
        here = pl.ds(pl.multiple_of(k * BLOCK, BLOCK), BLOCK)
        cell[:, :BLOCK] = work[k, :, here]
        row_b = lax.broadcasted_iota(jnp.int32, (BLOCK, BLOCK), 0)
        lane_b = lax.broadcasted_iota(jnp.int32, (BLOCK, BLOCK), 1)
        cell[:, BLOCK:] = (row_b == lane_b).astype(F32)

        def one_panel(p):
            base = p * PANEL
            left = cell[base:base + PANEL, :BLOCK]
            right = cell[base:base + PANEL, BLOCK:]
            spread = [jnp.broadcast_to(left[:, base + t:base + t + 1], (PANEL, BLOCK)) for t in range(PANEL)]
            scale = jnp.zeros((PANEL, BLOCK), F32)
            for t in range(PANEL):
                inv = 1.0 / jnp.broadcast_to(spread[t][t:t + 1, :], (PANEL, BLOCK))
                factor = jnp.where(sub > t, spread[t] * inv, 0.0)
                scale = jnp.where(sub == t, inv, scale)
                for later in range(t + 1, PANEL):
                    spread[later] = spread[later] - factor * jnp.broadcast_to(
                        spread[later][t:t + 1, :], (PANEL, BLOCK))
                left = left - factor * jnp.broadcast_to(left[t:t + 1, :], (PANEL, BLOCK))
                right = right - factor * jnp.broadcast_to(right[t:t + 1, :], (PANEL, BLOCK))
            weights = jnp.transpose(left * scale)
            for g in range(p + 1, (p // GROUP + 1) * GROUP):
                at = slice(g * PANEL, (g + 1) * PANEL)
                a, b = cell[at, :BLOCK], cell[at, BLOCK:]
                for t in range(PANEL):
                    w = jnp.broadcast_to(weights[at, t:t + 1], (PANEL, BLOCK))
                    a = a - w * jnp.broadcast_to(left[t:t + 1, :], (PANEL, BLOCK))
                    b = b - w * jnp.broadcast_to(right[t:t + 1, :], (PANEL, BLOCK))
                cell[at, :BLOCK] = a
                cell[at, BLOCK:] = b
            root = jnp.sqrt(scale)
            cell[base:base + PANEL, :BLOCK] = left * root
            cell[base:base + PANEL, BLOCK:] = right * root
            end = base + PANEL
            if end % (GROUP * PANEL) == 0 and end < BLOCK:
                done = cell[end - GROUP * PANEL:end, :]
                change = lax.dot_general(done[:, :BLOCK], done, (((0,), (0,)), ((), ())),
                                         precision=HIGHEST, preferred_element_type=F32)
                cell[end:, :] = cell[end:, :] - change[end:, :]

        sure = (real - (blocks - 1) * BLOCK + PANEL - 1) // PANEL
        for p in range(sure):
            one_panel(p)

        @pl.when(k < blocks - 1)
        def _():
            for p in range(sure, panels):
                one_panel(p)

        window = pl.ds(pl.multiple_of(k * BLOCK, BLOCK), size + BLOCK)
        mine = jnp.dot(cell[:, BLOCK:], work[k, :, window], precision=HIGHEST, preferred_element_type=F32)
        work[k, :, window] = mine

        @pl.when(k < blocks - 1)
        def _():
            change = lax.dot_general(mine[:, BLOCK:size], mine, (((0,), (0,)), ((), ())),
                                     precision=HIGHEST, preferred_element_type=F32)
            for n in range(blocks - 1):
                @pl.when(k + 1 + n < blocks)
                def _():
                    work[k + 1 + n, :, window] = work[k + 1 + n, :, window] - change[n * BLOCK:(n + 1) * BLOCK]

        return carry

    lax.fori_loop(0, blocks, block_step, 0)
    for k in range(blocks):
        count = min(BLOCK, real - k * BLOCK)
        at = slice(k * BLOCK, k * BLOCK + count)
        upper = jnp.where(lane >= row + k * BLOCK, work[k, :, :size], 0.0)
        upper_ref[at, :] = upper[:count, :real]
        inverse_ref[at, :] = work[k, :count, size:size + real]


def packed_blocks(gram):
    real = gram.shape[0]
    spare = -real % BLOCK
    gram = jnp.pad(gram, ((0, spare), (0, spare)))
    blocks = gram.shape[0] // BLOCK
    return jnp.concatenate([gram[i * BLOCK:(i + 1) * BLOCK, j * BLOCK:(j + 1) * BLOCK]
                            for i in range(blocks) for j in range(i, blocks)])


def factorize(packed, real):
    blocks = -(-real // BLOCK)
    size = blocks * BLOCK
    return pl.pallas_call(
        functools.partial(factor_kernel, real),
        out_shape=(jax.ShapeDtypeStruct((real, real), F32),) * 2,
        scratch_shapes=[pltpu.VMEM((blocks, BLOCK, 2 * size), F32), pltpu.VMEM((BLOCK, 2 * BLOCK), F32)],
        compiler_params=pltpu.CompilerParams(vmem_limit_bytes=60 << 20),
        name="factor",
    )(packed)


def solve_kernel(count, spots_ref, own_ref, inverse_ref, *refs):
    pieces, (out_ref, stage, value, sems) = refs[:count], refs[count:]
    copies = [pltpu.make_async_copy(piece, stage.at[spots_ref[s]], sems.at[s]) for s, piece in enumerate(pieces)]
    for copy in copies:
        copy.start()
    _, outer, cols = out_ref.shape
    low = inverse_ref[pl.ds(pl.multiple_of(own_ref[0] * cols, 8), cols), :]
    terms = []
    for _ in range(2):
        term = low.astype(BF16)
        low = low - term.astype(F32)
        terms.append(term)
    for copy in copies:
        copy.wait()
    rows = stage.shape[1]

    chunk = rows // SPLIT

    def one_part(n, carry):
        data = stage[n]
        product = sum(lax.dot_general(data, term, (((1,), (1,)), ((), ())), preferred_element_type=F32)
                      for term in terms)
        for s in range(SPLIT):
            at = (n // 2) * 2 * rows + (2 * s + n % 2) * chunk
            value[pl.ds(pl.multiple_of(at, 8), chunk), :] = product[s * chunk:(s + 1) * chunk]
        return carry

    lax.fori_loop(0, count, one_part, 0)
    pairs = outer // 2
    for d in range(BOND):
        for e in range(BOND):
            for i in range(2):
                data = value[pl.ds(d * 16 + i * 8 + e, pairs, stride=BOND * 16), :]
                out_ref[d * BOND + e, pl.ds(i, pairs, stride=2), :] = data


def solve(pieces, inverse, spots, own, cols):
    rows, width = pieces[0].shape
    outer = rows * len(pieces) // (BOND * 8)
    smem = pl.BlockSpec(memory_space=pltpu.SMEM)
    return pl.pallas_call(
        functools.partial(solve_kernel, len(pieces)),
        in_specs=[smem, smem, pl.BlockSpec(memory_space=pltpu.VMEM)] + [pl.BlockSpec(memory_space=pl.ANY)] * len(pieces),
        out_shape=jax.ShapeDtypeStruct((BOND * BOND, outer, cols), F32),
        scratch_shapes=[pltpu.VMEM((len(pieces), rows, width), BF16), pltpu.VMEM((rows * len(pieces), cols), F32),
                        pltpu.SemaphoreType.DMA((len(pieces),))],
        compiler_params=pltpu.CompilerParams(vmem_limit_bytes=60 << 20),
        name="solve",
    )(spots, own, inverse, *pieces)


def swap(x, mask):
    count = lax.axis_size("wide") * lax.axis_size("narrow")
    return lax.ppermute(x, ("wide", "narrow"), [(i, i ^ mask) for i in range(count)])


def bits_of(axis):
    return lax.axis_size(axis).bit_length() - 1


def gather_wide(x, after=()):
    if after:
        x = lax.optimization_barrier((x,) + tuple(after))[0]
    if lax.axis_size("wide") != 8:
        whole = lax.all_gather(x, "wide", axis=1, tiled=True)
        return [(0, 0, whole)], [whole]
    low = lax.axis_size("narrow")
    one, two, six = low, 2 * low, 6 * low
    blocks = {0: x, 1: swap(x, one), 2: swap(x, two), 6: swap(x, six)}
    blocks[3] = swap(blocks[2], one)
    blocks[4] = swap(blocks[6], two)
    blocks[7] = swap(blocks[1], six)
    blocks[5] = swap(blocks[4], one)
    return [(m, 0, blocks[m]) for m in range(8)], [blocks[3], blocks[5], blocks[7]]


def gather_narrow(x):
    blocks = [x]
    for bit in reversed(range(bits_of("narrow"))):
        blocks = blocks + [swap(b, 1 << bit) for b in blocks]
    return blocks


def narrow_masks():
    masks = [0]
    for bit in reversed(range(bits_of("narrow"))):
        masks = masks + [m | (1 << bit) for m in masks]
    return masks


def groups():
    bits = bits_of("narrow") + bits_of("wide")
    first = bits % 2
    out = [[1]] if first else []
    for b in range(first, bits, 2):
        out.append([1 << b, 2 << b])
    return out


def place_in(group, me):
    place, masks = 0, [0]
    for n, mask in enumerate(group):
        place = place + (((me // mask) % 2) << n)
        masks = masks + [m | mask for m in masks]
    return place, masks


def sum_group(x, group, me):
    place, masks = place_in(group, me)
    parts = x.reshape(len(masks), x.shape[0] // len(masks), x.shape[1])
    total = lax.dynamic_index_in_dim(parts, place, 0, False)
    for n, mask in list(enumerate(masks))[1:]:
        total = total + swap(lax.dynamic_index_in_dim(parts, place ^ n, 0, False), mask)
    return total


def join_group(x, group, me):
    place, masks = place_in(group, me)
    parts = jnp.stack([x] + [swap(x, mask) for mask in masks[1:]])
    return jnp.concatenate([lax.dynamic_index_in_dim(parts, place ^ n, 0, False) for n in range(len(masks))])


def move(left_edge, corner, right_edge, single_layer, warm_basis):
    local_rows, square, depth = left_edge.shape
    breadth = corner.shape[1]
    local_cols = right_edge.shape[2]
    narrow = lax.axis_size("narrow")
    own = lax.axis_index("narrow").astype(jnp.int32)
    me = lax.axis_index("wide").astype(jnp.int32) * narrow + own

    right, ahead = gather_wide(right_edge.transpose(1, 0, 2))
    lefts = [x.reshape(square * local_rows, depth) for x in gather_narrow(left_edge.transpose(1, 0, 2))]
    corners = gather_narrow(corner)
    half_left = half_left_of(lefts, corners, local_rows + -local_rows % OUTER)
    first, second = site_operands(single_layer)
    order = jnp.arange(shape_of(right)[0], dtype=jnp.int32)
    if len(right) > 1:
        order = order ^ (me // narrow)
    basis, _ = gather_wide(warm_basis.transpose(0, 2, 1), ahead)

    steps = half_left.shape[0] // TIGHT
    cuts = [0, 3, 5, steps] if steps > 5 else [0, steps]
    enlarged = None
    for n in range(len(cuts) - 1):
        made = enlarge(half_left, right, order, first, second, cuts[n], cuts[n + 1] - cuts[n], enlarged)
        enlarged = made[0]
        if n == 0:
            right = made[1]

    half = enlarged.shape[0] // 2
    spot = lambda *masks: jnp.stack([own ^ m for m in masks])

    def summed(mine, other):
        return mine.astype(F32) + swap(other, 1).astype(F32)

    place = lambda half: jnp.stack([half, own % 2])
    mine, other, basis = project(enlarged, basis, order, place(1 - own // 2), half, breadth)
    near = summed(mine, other).astype(BF16)
    enlarged, near = lax.optimization_barrier((enlarged, near))
    near = swap(near, 2)
    mine, other = project(enlarged, basis, order, place(own // 2), half, breadth)
    rows = (summed(mine, other) + near.astype(F32)).astype(BF16)

    gram = lax.dot_general(rows, rows, (((0,), (0,)), ((), ())), preferred_element_type=F32) / (breadth * square)
    gram = packed_blocks(gram)
    *halving, last = groups()
    for group in halving:
        gram = sum_group(gram, group, me)
    terms = [gram] + [swap(gram, mask) for mask in place_in(last, me)[1][1:]]
    while len(terms) > 1:
        terms = [a + b for a, b in zip(terms[::2], terms[1::2])]
    gram, = terms
    for group in reversed(halving):
        gram = join_group(gram, group, me)
    rows, gram = lax.optimization_barrier((rows, gram))
    pieces = gather_narrow(rows)
    upper, inverse = factorize(gram, breadth)
    new_basis = solve(pieces, inverse, spot(*narrow_masks()), own[None], local_cols)
    return new_basis.transpose(1, 0, 2)[:local_rows], upper


def solution(mesh):
    placed = (
        P("wide", None, "narrow"),
        P("narrow", None),
        P("wide", None, "narrow"),
        P(),
        P(None, "narrow", "wide"),
    )
    return jax.shard_map(
        move,
        mesh=mesh,
        in_specs=placed,
        out_specs=(P("wide", None, "narrow"), P()),
        check_vma=False,
    )
```

```python
import functools
import jax
import jax.numpy as jnp
from jax import lax
from jax.experimental import pallas as pl
from jax.experimental.pallas import tpu as pltpu
from jax.sharding import PartitionSpec as P


BOND = 7
LANES = 128
BLOCK = 128
PANEL = 8
GROUP = 8
OUTER = 8
ROWS = OUTER * 64
TIGHT = OUTER * BOND * 8
SPLIT = 7
F32 = jnp.float32
BF16 = jnp.bfloat16
HIGHEST = lax.Precision.HIGHEST


def site_operands(single_layer):
    phys = single_layer.shape[0]
    layer = single_layer.reshape(phys, BOND, BOND, BOND, BOND)
    half = 4
    padded = jnp.pad(layer, ((0, 0), (0, 1), (0, 0), (0, 0), (0, 0)))
    eye = jnp.eye(half, dtype=layer.dtype)
    first = padded.transpose(3, 4, 0, 2, 1)[:, :, :, None, :, None, :] * eye[None, None, None, :, None, :, None]
    first = first.reshape(BOND * BOND * phys * half, BOND * half * 8)
    split = padded.reshape(phys, 2, half, BOND, BOND, BOND)
    second = jnp.pad(split.transpose(5, 4, 3, 1, 0, 2), ((0, 0), (0, 1), (0, 0), (0, 0), (0, 0), (0, 0)))
    return first, second.reshape(BOND * 8, BOND * 2 * phys * half)


def assemble(layout, order_ref, pieces, stage, target, sems):
    copies = [pltpu.make_async_copy(piece, stage.at[block, pl.ds(begin, size)], sems.at[s])
              for s, ((block, begin, size), piece) in enumerate(zip(layout, pieces))]
    for copy in copies:
        copy.start()
    target[...] = jnp.zeros_like(target)
    for copy in copies:
        copy.wait()
    count, square, depth, breadth = stage.shape

    def fill(q, carry):
        lane = pl.ds(pl.multiple_of(q * LANES, LANES), breadth)
        if count == 1:
            target[:, lane] = stage[0, q]
        for pair in range(count // 2):
            joined = jnp.concatenate(
                [stage[order_ref[2 * pair + k], q].astype(F32) for k in range(2)], axis=0)
            target[pl.ds(pair * 2 * depth, 2 * depth), lane] = joined.astype(BF16)
        return carry

    lax.fori_loop(0, square, fill, 0, unroll=BOND)


def half_left_kernel(parts_of, *refs):
    left_refs, corner_refs = refs[:parts_of], refs[parts_of:2 * parts_of]
    out_ref, total, spread = refs[2 * parts_of:]
    value = jnp.dot(left_refs[0][...], corner_refs[0][...], preferred_element_type=F32)
    for n in range(1, parts_of):
        value += jnp.dot(left_refs[n][...], corner_refs[n][...], preferred_element_type=F32)
    outer = total.shape[0] // (BOND * BOND)
    spread[...] = jnp.zeros_like(spread)
    width = value.shape[1]
    total[:, :width] = value

    def place(u, v):
        begin = (u * BOND + v) * outer
        if outer % 8 == 0:
            begin = pl.multiple_of(begin, 8)
        for c in range(spread.shape[0]):
            data = total[pl.ds(begin, outer), c * LANES:(c + 1) * LANES]
            spread[c, pl.ds(v * 8 + u, outer, stride=BOND * 8), :] = data

    if outer % 8 == 0:
        lax.fori_loop(0, BOND * BOND, lambda p, carry: (place(p // BOND, p % BOND), carry)[1], 0)
    else:
        for p in range(BOND * BOND):
            place(p // BOND, p % BOND)
    for c in range(spread.shape[0]):
        count = min(LANES, width - c * LANES)
        out_ref[:, c * LANES:c * LANES + count] = spread[c, :, :count].astype(BF16)


def half_left_of(lefts, corners, outer):
    width = corners[0].shape[1]
    return pl.pallas_call(
        functools.partial(half_left_kernel, len(lefts)),
        out_shape=jax.ShapeDtypeStruct((outer * BOND * 8, width), BF16),
        scratch_shapes=[pltpu.VMEM((lefts[0].shape[0], -(-width // LANES) * LANES), F32),
                        pltpu.VMEM((-(-width // LANES), outer * BOND * 8, LANES), F32)],
        compiler_params=pltpu.CompilerParams(vmem_limit_bytes=60 << 20),
        name="half_left",
    )(*lefts, *corners)


def enlarge_kernel(layout, order_ref, half_ref, first_ref, second_ref, *rest):
    count = len(layout)
    if count:
        pieces, (out_ref, right_all, stage, strip, ket, sems) = rest[:count], rest[count:]

        @pl.when(pl.program_id(0) == 0)
        def _():
            assemble(layout, order_ref, pieces, stage, right_all, sems)
    else:
        right_all, _, out_ref, strip, ket = rest
    rows = strip.shape[1]
    square = BOND * BOND
    span = BOND * LANES
    half_left = half_ref[...]
    for l in range(BOND):
        value = jnp.dot(half_left, right_all[:, l * span:(l + 1) * span], preferred_element_type=F32)
        value = jnp.concatenate([value.reshape(OUTER, BOND * 8, span), jnp.zeros((OUTER, 8, span), F32)], axis=1)
        strip[l] = value.astype(BF16).reshape(rows, span)

    def one_pair(pair, carry):
        for i in range(2):
            parts = []
            for g in range(2):
                at = pl.ds(pl.multiple_of((pair * 2 + i) * 64 + g * 32, 32), 32)
                data = strip[:, at, :].reshape(BOND * 32, span)
                part = jnp.dot(first_ref[...], data, preferred_element_type=F32)
                parts.append(part.reshape(square, 8, span))
            ket[i] = jnp.concatenate(parts, axis=1).astype(BF16)
        for d in range(BOND):
            rows_of = []
            for lp in range(BOND):
                rows_of.append(jnp.concatenate(
                    [ket[i, d * BOND + r, :, lp * LANES:(lp + 1) * LANES] for r in range(BOND) for i in range(2)],
                    axis=1))
            data = jnp.concatenate(rows_of, axis=0)
            value = jnp.dot(second_ref[...], data, preferred_element_type=F32)
            at = pl.ds(pl.multiple_of((pair * BOND + d) * 16, 16), 16)
            for r in range(BOND):
                two = [value[:, (r * 2 + i) * LANES:(r * 2 + i + 1) * LANES].reshape(BOND, 8, LANES)
                       for i in range(2)]
                both = jnp.concatenate(two, axis=1).astype(BF16)
                for rp in range(BOND):
                    out_ref[at, (r * BOND + rp) * LANES:(r * BOND + rp + 1) * LANES] = both[rp]
        return carry

    lax.fori_loop(0, rows // 128, one_pair, 0)


def whole_block(a):
    return pl.BlockSpec(a.shape, lambda s: (0,) * a.ndim, pipeline_mode=pl.Buffered(1))


def shape_of(pieces):
    blocks = 1 + max(block for block, _, _ in pieces)
    square = sum(piece.shape[0] for block, _, piece in pieces if block == 0)
    return (blocks, square) + pieces[0][2].shape[1:]


def layout_of(pieces):
    return tuple((block, begin, piece.shape[0]) for block, begin, piece in pieces)


def enlarge(half_left, right, order, first, second, begin, steps, before=None):
    total, depth = half_left.shape
    pieces = right if isinstance(right, list) else None
    square = BOND * BOND
    lanes = square * LANES
    out_rows = ROWS // 128 * BOND * 16
    in_specs = [pl.BlockSpec(memory_space=pltpu.SMEM), pl.BlockSpec((TIGHT, depth), lambda s: (s + begin, 0)),
                whole_block(first), whole_block(second)]
    out_specs = [pl.BlockSpec((out_rows, lanes), lambda s: (s + begin, 0))]
    out_shape = [jax.ShapeDtypeStruct((total // TIGHT * out_rows, lanes), BF16)]
    scratch = [pltpu.VMEM((BOND, ROWS, BOND * LANES), BF16), pltpu.VMEM((2, square, 16, BOND * LANES), BF16)]
    if pieces:
        shape = shape_of(pieces)
        width = shape[0] * shape[2]
        in_specs += [pl.BlockSpec(memory_space=pl.ANY)] * len(pieces)
        out_specs.append(pl.BlockSpec((width, lanes), lambda s: (0, 0), pipeline_mode=pl.Buffered(1)))
        out_shape.append(jax.ShapeDtypeStruct((width, lanes), BF16))
        scratch = [pltpu.VMEM(shape, BF16)] + scratch
        scratch.append(pltpu.SemaphoreType.DMA((len(pieces),)))
    else:
        in_specs += [whole_block(right), pl.BlockSpec(memory_space=pl.ANY)]
    flops = 2 * steps * ROWS * lanes * 1024
    return pl.pallas_call(
        functools.partial(enlarge_kernel, layout_of(pieces) if pieces else ()),
        grid=(steps,),
        in_specs=in_specs,
        out_specs=out_specs,
        out_shape=out_shape,
        scratch_shapes=scratch,
        compiler_params=pltpu.CompilerParams(dimension_semantics=("arbitrary",), vmem_limit_bytes=60 << 20),
        cost_estimate=pl.CostEstimate(flops=flops, transcendentals=0, bytes_accessed=steps * out_rows * lanes * 2),
        input_output_aliases={} if pieces else {len(in_specs) - 1: 0},
        name="enlarge",
    )(order, half_left, first, second, *([p for _, _, p in pieces] if pieces else [right, before]))


def project_kernel(layout, order_ref, spot_ref, rows_ref, *refs):
    count = len(layout)
    if count:
        pieces, (mine_ref, other_ref, basis_all, stage, sems) = refs[:count], refs[count:]

        @pl.when(pl.program_id(0) == 0)
        def _():
            assemble(layout, order_ref, pieces, stage, basis_all, sems)
    else:
        basis_all, mine_ref, other_ref = refs
    value = lax.dot_general(rows_ref[...], basis_all[...], (((1,), (1,)), ((), ())),
                            preferred_element_type=F32).astype(BF16)
    chunk = value.shape[0] // 2
    for upper, (low_ref, high_ref) in enumerate(((mine_ref, other_ref), (other_ref, mine_ref))):
        @pl.when(spot_ref[1] == upper)
        def _():
            low_ref[...] = value[:chunk]
            high_ref[...] = value[chunk:]


def project(enlarged, basis, order, spot, rows, width):
    lanes = enlarged.shape[1]
    pieces = basis if isinstance(basis, list) else None
    once = rows // SPLIT
    full = lambda shape: pl.BlockSpec(shape, lambda s, order, spot: (0,) * len(shape), pipeline_mode=pl.Buffered(1))
    in_specs = [pl.BlockSpec((once, lanes), lambda s, order, spot: (spot[0] * SPLIT + s, 0))]
    out_specs = [pl.BlockSpec((once // 2, width), lambda s, order, spot: (s, 0))] * 2
    out_shape = [jax.ShapeDtypeStruct((rows // 2, width), BF16)] * 2
    scratch = []
    if pieces:
        in_specs += [pl.BlockSpec(memory_space=pl.ANY)] * len(pieces)
        out_specs.append(full((width, lanes)))
        out_shape.append(jax.ShapeDtypeStruct((width, lanes), BF16))
        scratch += [pltpu.VMEM(shape_of(pieces), BF16), pltpu.SemaphoreType.DMA((len(pieces),))]
    else:
        in_specs.append(full(basis.shape))
    return pl.pallas_call(
        functools.partial(project_kernel, layout_of(pieces) if pieces else ()),
        grid_spec=pltpu.PrefetchScalarGridSpec(
            num_scalar_prefetch=2, grid=(SPLIT,), in_specs=in_specs, out_specs=out_specs, scratch_shapes=scratch),
        out_shape=out_shape,
        compiler_params=pltpu.CompilerParams(dimension_semantics=("arbitrary",), vmem_limit_bytes=60 << 20),
        cost_estimate=pl.CostEstimate(flops=2 * rows * width * lanes, transcendentals=0,
                                      bytes_accessed=2 * rows * lanes),
        name="project",
    )(order, spot, enlarged, *([p for _, _, p in pieces] if pieces else [basis]))


def factor_kernel(real, gram_ref, upper_ref, inverse_ref, work, cell):
    blocks = work.shape[0]
    size = blocks * BLOCK
    lane = lax.broadcasted_iota(jnp.int32, (BLOCK, size), 1)
    row = lax.broadcasted_iota(jnp.int32, (BLOCK, size), 0)
    place = 0
    for k in range(blocks):
        unit = (lane == row + k * BLOCK).astype(F32)
        work[k, :, :size] = jnp.where(lane >= real, unit, 0.0)
        work[k, :, size:] = unit
        narrow = paired(real)
        for j in range(k, blocks - narrow):
            at = slice(j * BLOCK, (j + 1) * BLOCK)
            work[k, :, at] = work[k, :, at] + gram_ref[place * BLOCK:(place + 1) * BLOCK, :]
            place += 1
    if paired(real):
        half = BLOCK // 2
        for k in range(blocks):
            data = gram_ref[(place + k // 2) * BLOCK:(place + k // 2 + 1) * BLOCK, :]
            work[k, :, size - BLOCK:size - half] = data[:, k % 2 * half:(k % 2 + 1) * half]
    sub = lax.broadcasted_iota(jnp.int32, (PANEL, BLOCK), 0)
    lane8 = lax.broadcasted_iota(jnp.int32, (PANEL, BLOCK), 1)
    panels = BLOCK // PANEL

    def block_step(k, carry):
        here = pl.ds(pl.multiple_of(k * BLOCK, BLOCK), BLOCK)
        cell[:, :BLOCK] = work[k, :, here]
        row_b = lax.broadcasted_iota(jnp.int32, (BLOCK, BLOCK), 0)
        lane_b = lax.broadcasted_iota(jnp.int32, (BLOCK, BLOCK), 1)
        cell[:, BLOCK:] = (row_b == lane_b).astype(F32)

        def one_panel(p):
            base = p * PANEL
            left = cell[base:base + PANEL, :BLOCK]
            right = cell[base:base + PANEL, BLOCK:]
            spread = [jnp.broadcast_to(left[:, base + t:base + t + 1], (PANEL, BLOCK)) for t in range(PANEL)]
            scale = jnp.zeros((PANEL, BLOCK), F32)
            for t in range(PANEL):
                inv = 1.0 / jnp.broadcast_to(spread[t][t:t + 1, :], (PANEL, BLOCK))
                factor = jnp.where(sub > t, spread[t] * inv, 0.0)
                scale = jnp.where(sub == t, inv, scale)
                for later in range(t + 1, PANEL):
                    spread[later] = spread[later] - factor * jnp.broadcast_to(
                        spread[later][t:t + 1, :], (PANEL, BLOCK))
                left = left - factor * jnp.broadcast_to(left[t:t + 1, :], (PANEL, BLOCK))
                right = right - factor * jnp.broadcast_to(right[t:t + 1, :], (PANEL, BLOCK))
            weights = jnp.transpose(left * scale)
            for g in range(p + 1, (p // GROUP + 1) * GROUP):
                at = slice(g * PANEL, (g + 1) * PANEL)
                a, b = cell[at, :BLOCK], cell[at, BLOCK:]
                for t in range(PANEL):
                    w = jnp.broadcast_to(weights[at, t:t + 1], (PANEL, BLOCK))
                    a = a - w * jnp.broadcast_to(left[t:t + 1, :], (PANEL, BLOCK))
                    b = b - w * jnp.broadcast_to(right[t:t + 1, :], (PANEL, BLOCK))
                cell[at, :BLOCK] = a
                cell[at, BLOCK:] = b
            root = jnp.sqrt(scale)
            cell[base:base + PANEL, :BLOCK] = left * root
            cell[base:base + PANEL, BLOCK:] = right * root
            end = base + PANEL
            if end % (GROUP * PANEL) == 0 and end < BLOCK:
                done = cell[end - GROUP * PANEL:end, :]
                change = lax.dot_general(done[:, :BLOCK], done, (((0,), (0,)), ((), ())),
                                         precision=HIGHEST, preferred_element_type=F32)
                cell[end:, :] = cell[end:, :] - change[end:, :]

        sure = (real - (blocks - 1) * BLOCK + PANEL - 1) // PANEL
        for p in range(sure):
            one_panel(p)

        @pl.when(k < blocks - 1)
        def _():
            for p in range(sure, panels):
                one_panel(p)

        window = pl.ds(pl.multiple_of(k * BLOCK, BLOCK), size + BLOCK)
        mine = jnp.dot(cell[:, BLOCK:], work[k, :, window], precision=HIGHEST, preferred_element_type=F32)
        work[k, :, window] = mine

        @pl.when(k < blocks - 1)
        def _():
            change = lax.dot_general(mine[:, BLOCK:size], mine, (((0,), (0,)), ((), ())),
                                     precision=HIGHEST, preferred_element_type=F32)
            for n in range(blocks - 1):
                @pl.when(k + 1 + n < blocks)
                def _():
                    work[k + 1 + n, :, window] = work[k + 1 + n, :, window] - change[n * BLOCK:(n + 1) * BLOCK]

        return carry

    lax.fori_loop(0, blocks, block_step, 0)
    for k in range(blocks):
        count = min(BLOCK, real - k * BLOCK)
        at = slice(k * BLOCK, k * BLOCK + count)
        upper = jnp.where(lane >= row + k * BLOCK, work[k, :, :size], 0.0)
        upper_ref[at, :] = upper[:count, :real]
        inverse_ref[at, :] = work[k, :count, size:size + real]


def paired(real):
    return real % BLOCK == BLOCK // 2 and -(-real // BLOCK) % 2 == 0


def packed_blocks(gram):
    real = gram.shape[0]
    spare = -real % BLOCK
    gram = jnp.pad(gram, ((0, spare), (0, spare)))
    blocks = gram.shape[0] // BLOCK
    narrow = paired(real)
    block = lambda i, j, width: gram[i * BLOCK:(i + 1) * BLOCK, j * BLOCK:j * BLOCK + width]
    whole = [block(i, j, BLOCK) for i in range(blocks) for j in range(i, blocks - narrow)]
    if narrow:
        whole += [jnp.concatenate([block(i + n, blocks - 1, BLOCK // 2) for n in range(2)], axis=1)
                  for i in range(0, blocks, 2)]
    return jnp.concatenate(whole)


def factorize(packed, real):
    blocks = -(-real // BLOCK)
    size = blocks * BLOCK
    return pl.pallas_call(
        functools.partial(factor_kernel, real),
        out_shape=(jax.ShapeDtypeStruct((real, real), F32),) * 2,
        scratch_shapes=[pltpu.VMEM((blocks, BLOCK, 2 * size), F32), pltpu.VMEM((BLOCK, 2 * BLOCK), F32)],
        compiler_params=pltpu.CompilerParams(vmem_limit_bytes=60 << 20),
        name="factor",
    )(packed)


def solve_kernel(count, spots_ref, own_ref, inverse_ref, *refs):
    pieces, (out_ref, stage, value, sems) = refs[:count], refs[count:]
    copies = [pltpu.make_async_copy(piece, stage.at[spots_ref[s]], sems.at[s]) for s, piece in enumerate(pieces)]
    for copy in copies:
        copy.start()
    _, outer, cols = out_ref.shape
    low = inverse_ref[pl.ds(pl.multiple_of(own_ref[0] * cols, 8), cols), :]
    terms = []
    for _ in range(2):
        term = low.astype(BF16)
        low = low - term.astype(F32)
        terms.append(term)
    for copy in copies:
        copy.wait()
    rows = stage.shape[1]

    chunk = rows // SPLIT

    def one_part(n, carry):
        data = stage[n]
        product = sum(lax.dot_general(data, term, (((1,), (1,)), ((), ())), preferred_element_type=F32)
                      for term in terms)
        for s in range(SPLIT):
            at = (n // 2) * 2 * rows + (2 * s + n % 2) * chunk
            value[pl.ds(pl.multiple_of(at, 8), chunk), :] = product[s * chunk:(s + 1) * chunk]
        return carry

    lax.fori_loop(0, count, one_part, 0)
    pairs = outer // 2
    for d in range(BOND):
        for e in range(BOND):
            for i in range(2):
                data = value[pl.ds(d * 16 + i * 8 + e, pairs, stride=BOND * 16), :]
                out_ref[d * BOND + e, pl.ds(i, pairs, stride=2), :] = data


def solve(pieces, inverse, spots, own, cols):
    rows, width = pieces[0].shape
    outer = rows * len(pieces) // (BOND * 8)
    smem = pl.BlockSpec(memory_space=pltpu.SMEM)
    return pl.pallas_call(
        functools.partial(solve_kernel, len(pieces)),
        in_specs=[smem, smem, pl.BlockSpec(memory_space=pltpu.VMEM)] + [pl.BlockSpec(memory_space=pl.ANY)] * len(pieces),
        out_shape=jax.ShapeDtypeStruct((BOND * BOND, outer, cols), F32),
        scratch_shapes=[pltpu.VMEM((len(pieces), rows, width), BF16), pltpu.VMEM((rows * len(pieces), cols), F32),
                        pltpu.SemaphoreType.DMA((len(pieces),))],
        compiler_params=pltpu.CompilerParams(vmem_limit_bytes=60 << 20),
        name="solve",
    )(spots, own, inverse, *pieces)


def swap(x, mask):
    count = lax.axis_size("wide") * lax.axis_size("narrow")
    return lax.ppermute(x, ("wide", "narrow"), [(i, i ^ mask) for i in range(count)])


def bits_of(axis):
    return lax.axis_size(axis).bit_length() - 1


def gather_wide(x, after=()):
    if after:
        x = lax.optimization_barrier((x,) + tuple(after))[0]
    if lax.axis_size("wide") != 8:
        whole = lax.all_gather(x, "wide", axis=1, tiled=True)
        return [(0, 0, whole)], [whole]
    low = lax.axis_size("narrow")
    one, two, six = low, 2 * low, 6 * low
    blocks = {0: x, 1: swap(x, one), 2: swap(x, two), 6: swap(x, six)}
    blocks[3] = swap(blocks[2], one)
    blocks[4] = swap(blocks[6], two)
    blocks[7] = swap(blocks[1], six)
    blocks[5] = swap(blocks[4], one)
    return [(m, 0, blocks[m]) for m in range(8)], [blocks[3], blocks[5], blocks[7]]


def gather_narrow(x):
    blocks = [x]
    for bit in reversed(range(bits_of("narrow"))):
        blocks = blocks + [swap(b, 1 << bit) for b in blocks]
    return blocks


def narrow_masks():
    masks = [0]
    for bit in reversed(range(bits_of("narrow"))):
        masks = masks + [m | (1 << bit) for m in masks]
    return masks


def groups():
    bits = bits_of("narrow") + bits_of("wide")
    first = bits % 2
    out = [[1]] if first else []
    for b in range(first, bits, 2):
        out.append([1 << b, 2 << b])
    return out


def place_in(group, me):
    place, masks = 0, [0]
    for n, mask in enumerate(group):
        place = place + (((me // mask) % 2) << n)
        masks = masks + [m | mask for m in masks]
    return place, masks


def sum_group(x, group, me):
    place, masks = place_in(group, me)
    parts = x.reshape(len(masks), x.shape[0] // len(masks), x.shape[1])
    total = lax.dynamic_index_in_dim(parts, place, 0, False)
    for n, mask in list(enumerate(masks))[1:]:
        total = total + swap(lax.dynamic_index_in_dim(parts, place ^ n, 0, False), mask)
    return total


def join_group(x, group, me):
    place, masks = place_in(group, me)
    parts = jnp.stack([x] + [swap(x, mask) for mask in masks[1:]])
    return jnp.concatenate([lax.dynamic_index_in_dim(parts, place ^ n, 0, False) for n in range(len(masks))])


def move(left_edge, corner, right_edge, single_layer, warm_basis):
    local_rows, square, depth = left_edge.shape
    breadth = corner.shape[1]
    local_cols = right_edge.shape[2]
    narrow = lax.axis_size("narrow")
    own = lax.axis_index("narrow").astype(jnp.int32)
    me = lax.axis_index("wide").astype(jnp.int32) * narrow + own

    right, ahead = gather_wide(right_edge.transpose(1, 0, 2))
    lefts = [x.reshape(square * local_rows, depth) for x in gather_narrow(left_edge.transpose(1, 0, 2))]
    corners = gather_narrow(corner)
    half_left = half_left_of(lefts, corners, local_rows + -local_rows % OUTER)
    first, second = site_operands(single_layer)
    order = jnp.arange(shape_of(right)[0], dtype=jnp.int32)
    if len(right) > 1:
        order = order ^ (me // narrow)
    basis, _ = gather_wide(warm_basis.transpose(0, 2, 1), ahead)

    steps = half_left.shape[0] // TIGHT
    cuts = [0, 3, 5, steps] if steps > 5 else [0, steps]
    enlarged = None
    for n in range(len(cuts) - 1):
        made = enlarge(half_left, right, order, first, second, cuts[n], cuts[n + 1] - cuts[n], enlarged)
        enlarged = made[0]
        if n == 0:
            right = made[1]

    half = enlarged.shape[0] // 2
    spot = lambda *masks: jnp.stack([own ^ m for m in masks])

    def summed(mine, other):
        return mine.astype(F32) + swap(other, 1).astype(F32)

    place = lambda half: jnp.stack([half, own % 2])
    mine, other, basis = project(enlarged, basis, order, place(1 - own // 2), half, breadth)
    near = summed(mine, other).astype(BF16)
    enlarged, near = lax.optimization_barrier((enlarged, near))
    near = swap(near, 2)
    mine, other = project(enlarged, basis, order, place(own // 2), half, breadth)
    rows = (summed(mine, other) + near.astype(F32)).astype(BF16)

    gram = lax.dot_general(rows, rows, (((0,), (0,)), ((), ())), preferred_element_type=F32) / (breadth * square)
    gram = packed_blocks(gram)
    *halving, last = groups()
    for group in halving:
        gram = sum_group(gram, group, me)
    terms = [gram] + [swap(gram, mask) for mask in place_in(last, me)[1][1:]]
    while len(terms) > 1:
        terms = [a + b for a, b in zip(terms[::2], terms[1::2])]
    gram, = terms
    for group in reversed(halving):
        gram = join_group(gram, group, me)
    rows, gram = lax.optimization_barrier((rows, gram))
    pieces = gather_narrow(rows)
    upper, inverse = factorize(gram, breadth)
    new_basis = solve(pieces, inverse, spot(*narrow_masks()), own[None], local_cols)
    return new_basis.transpose(1, 0, 2)[:local_rows], upper


def solution(mesh):
    placed = (
        P("wide", None, "narrow"),
        P("narrow", None),
        P("wide", None, "narrow"),
        P(),
        P(None, "narrow", "wide"),
    )
    return jax.shard_map(
        move,
        mesh=mesh,
        in_specs=placed,
        out_specs=(P("wide", None, "narrow"), P()),
        check_vma=False,
    )
```
